512 devices in a mesh: span: 16 (over z_hi, x), wall: 16 (over y, core), stream: 2 (over z_lo).
Axes of the slice: x: 4, y: 8, z: 8 (z_hi: 4, z_lo: 2; z = z_hi * 2 + z_lo), core: 2. Of those that a mesh axis runs over, the one named last changes fastest.
Arguments:
- fields: float32 [4, 16, 256, 2048], P(None, 'stream', 'wall', 'span'), may hold values from -67.5 to 67.5, as said below
Outputs:
- clark_model: float32 [3, 16, 256, 2048], P(None, 'stream', 'wall', 'span')
- similar_model: float32 [3, 16, 256, 2048], P(None, 'stream', 'wall', 'span')
- clark_corr: float32 [3, 256], P(None, 'wall')
- similar_corr: float32 [3, 256], P(None, 'wall')
The draws below stay inside these ranges and needn't reach their ends.
Inputs may be any that keep to these rules, and one draw needn't show every extreme that they name: The fields are rough from cell to cell.
All inputs are finite; a program needn't handle non-finite values.
Results may differ from the reference program's by a relative error of at most 0.00024.
Values sent between devices are 32-bit elements; how exact they have to be, the bound alone decides.
A program may use at most 64 MiB of HBM per device.

```python
import math
import jax
import jax.numpy as jnp
from jax import lax

NS = 16
NW = 256
NP = 2048


def draw_fields(key, part):
    first_key, second_key = jax.random.split(key)
    shape = (4, NS, NW, NP)
    spanwise = jnp.arange(NP, dtype=jnp.float32)
    base = jnp.clip(jax.random.normal(first_key, shape, jnp.float32), -5.0, 5.0)
    rough = jax.random.uniform(second_key, shape, jnp.float32, 0.5, 1.5)
    ramp = 1.0 + 2.0 * spanwise / max(NP - 1, 1)
    return 3.0 * base * rough * ramp[None, None, None, :]


def setup_inputs(seed: int = 0) -> dict:
    keys = jax.random.split(jax.random.key(seed), 2)
    return {
        "fields": draw_fields(jax.random.fold_in(keys[1], 71), 0),
    }


raw_taps = [math.exp(-(k - 8) ** 2 / 18.0) for k in range(17)]
filter_taps = [value / sum(raw_taps) for value in raw_taps]
clark_coef = 9.0
small_eps = 1e-06

def smooth(padded, direction, length):
    result = filter_taps[0] * lax.slice_in_dim(padded, 0, length, axis=direction)
    for k in range(1, 17):
        result = result + filter_taps[k] * lax.slice_in_dim(padded, k, k + length, axis=direction)
    return result

def filter_one(field):
    padded = jnp.pad(field, ((0, 0), (0, 0), (8, 8)), mode='wrap')
    field = smooth(padded, 2, NP)
    padded = jnp.pad(field, ((0, 0), (8, 8), (0, 0)))
    field = smooth(padded, 1, NW)
    padded = jnp.pad(field, ((8, 8), (0, 0), (0, 0)))
    return smooth(padded, 0, NS)

def with_products(quad):
    return jnp.concatenate([quad, quad[:3] * quad[3:4]], axis=0)

def filter_all(quad):
    return lax.map(filter_one, with_products(quad))

def clark_flux(means):
    padded = jnp.pad(means, ((0, 0), (0, 0), (0, 0), (1, 1)), mode='wrap')
    along_span = (padded[..., 2:] - padded[..., :-2]) * 0.5
    padded = jnp.pad(means, ((0, 0), (0, 0), (1, 1), (0, 0)))
    along_wall = (padded[:, :, 2:, :] - padded[:, :, :-2, :]) * 0.5
    padded = jnp.pad(means, ((0, 0), (1, 1), (0, 0), (0, 0)))
    along_stream = (padded[:, 2:] - padded[:, :-2]) * 0.5
    total = along_span[:3] * along_span[3:4] + along_wall[:3] * along_wall[3:4]
    total = total + along_stream[:3] * along_stream[3:4]
    return clark_coef * total

def reference(fields):
    first = filter_all(fields)
    means = first[:4]
    exact = first[4:] - means[:3] * means[3:4]
    second = filter_all(means)
    similar = second[4:] - second[:3] * second[3:4]
    clark = clark_flux(means)
    plane_cells = float(NS * NP)
    cross_c = lax.optimization_barrier(jnp.sum(exact * clark, axis=(1, 3))) / plane_cells
    cross_s = lax.optimization_barrier(jnp.sum(exact * similar, axis=(1, 3))) / plane_cells
    power_e = lax.optimization_barrier(jnp.sum(exact * exact, axis=(1, 3))) / plane_cells
    power_c = lax.optimization_barrier(jnp.sum(clark * clark, axis=(1, 3))) / plane_cells
    power_s = lax.optimization_barrier(jnp.sum(similar * similar, axis=(1, 3))) / plane_cells
    clark_corr = cross_c / jnp.sqrt((power_e + small_eps) * (power_c + small_eps))
    similar_corr = cross_s / jnp.sqrt((power_e + small_eps) * (power_s + small_eps))
    clark_model = clark / jnp.sqrt(power_c + small_eps)[:, None, :, None]
    similar_model = similar / jnp.sqrt(power_s + small_eps)[:, None, :, None]
    return (clark_model, similar_model, clark_corr, similar_corr)
```

```python
import math

import jax
import jax.numpy as jnp
import ml_dtypes
import numpy as np
from jax import lax
from jax.experimental import pallas as pl
from jax.experimental.pallas import tpu as pltpu
from jax.sharding import PartitionSpec as P

raw_taps = [math.exp(-((k - 8) ** 2) / 18.0) for k in range(17)]
filter_taps = [value / sum(raw_taps) for value in raw_taps]
clark_coef = 9.0
small_eps = 1e-06

MESH = pl.DeviceIdType.MESH
BF = jnp.bfloat16
F32 = jnp.float32
ROW = 4
NQ = 5


def tap(out_at, in_at):
    offset = in_at - out_at + 8
    inside = (offset >= 0) & (offset <= 16)
    return np.where(inside, np.array(filter_taps)[np.clip(offset, 0, 16)], 0.0)


def split(matrix):
    full = matrix.astype(np.float32)
    hi = full.astype(ml_dtypes.bfloat16)
    lo = (full - hi.astype(np.float32)).astype(ml_dtypes.bfloat16)
    return hi, lo


def left_stack(matrix):
    hi, lo = split(matrix)
    return np.concatenate([hi, hi, lo], axis=1)


def right_stack(matrix):
    hi, lo = split(matrix)
    return np.concatenate([hi, hi, lo], axis=0)


def plane_matrices():
    s_out, w_out = np.meshgrid(np.arange(16), np.arange(16), indexing="ij")
    s_out, w_out = s_out.reshape(-1, 1), w_out.reshape(-1, 1)
    b, s, w = np.meshgrid(np.arange(2), np.arange(16), np.arange(16), indexing="ij")
    blocks = tap(s_out, s.reshape(1, -1)) * tap(w_out + 8, (b * 16 + w).reshape(1, -1))
    s, w = np.meshgrid(np.arange(16), np.arange(32), indexing="ij")
    rows = tap(s_out, s.reshape(1, -1)) * tap(w_out + 8, w.reshape(1, -1))
    own = np.stack([left_stack(rows[:128]), left_stack(rows[128:])])
    return left_stack(blocks), own


def span_matrices():
    lane = np.arange(128)
    group, inner = lane // 32, lane % 32
    place = np.where(inner < 16, inner - 16, inner + 112)
    kept = (inner >= 8) & (inner < 24)
    main = tap(lane[None, :], lane[:, None])
    result = []
    for f in range(4):
        from_rim = tap(lane[None, :], place[:, None]) * (group == f)[:, None]
        to_rim = tap(place[None, :], lane[:, None]) * ((group == f) & kept)[None, :]
        rim = tap(place[None, :], place[:, None]) * (group[:, None] == group[None, :])
        rim = rim * kept[None, :] * (1.0 if f == 0 else 0.0)
        result.append(right_stack(np.block([[main, to_rim], [from_rim, rim]])))
    return np.stack(result)


def hi_lo(values):
    hi = values.astype(BF)
    return hi, (values - hi.astype(F32)).astype(BF)


def rim_product(rims):
    lane = lax.broadcasted_iota(jnp.int32, rims.shape, 1)
    last = jnp.where(lane >= 96, rims, 0.0)
    last = last + pltpu.roll(last, 32, 1)
    last = last + pltpu.roll(last, 64, 1)
    return rims * last


def kernel(
    cells, fields, km_in, ko_in, w_in,
    clark_out, similar_out, cc_out, sc_out,
    x, edge, edge_in, km, ko, wm, yh, yl, m, mh, zs, st, st_a, st_t, st_b,
    loc, z_s, z_r, own_s, own_r, rel_s, rel_r, e_s, e_r, a_s, a_r, b_s, b_r,
):
    p, wl, s = lax.axis_index("span"), lax.axis_index("wall"), lax.axis_index("stream")
    np_, nw = lax.axis_size("span"), lax.axis_size("wall")
    nz = np_ // ROW
    xi, zi = p % ROW, p // ROW
    o = 1 - s
    mine = pl.multiple_of(s * 8, 8)
    theirs = pl.multiple_of(o * 8, 8)

    greet = [{"span": (p + 1) % np_}, {"span": (p + np_ - 1) % np_}]
    greet += [{"wall": (wl + 1) % nw}, {"wall": (wl + nw - 1) % nw}]
    row_mates = [
        {"span": zi * ROW + (xi + k // 2) % ROW, "stream": (s + k % 2) % 2}
        for k in range(1, 2 * ROW)
    ]
    col_mates = [{"span": ((zi + k) % nz) * ROW + xi} for k in range(1, nz)]
    greet += row_mates + col_mates

    local = [
        pltpu.make_async_copy(fields.at[f], x.at[f, 1, pl.ds(mine, 8)], loc.at[f])
        for f in range(4)
    ]
    local += [
        pltpu.make_async_copy(km_in, km, loc.at[4]),
        pltpu.make_async_copy(ko_in.at[s], ko, loc.at[5]),
        pltpu.make_async_copy(w_in, wm, loc.at[6]),
    ]
    for copy in local:
        copy.start()

    barrier = pltpu.get_barrier_semaphore()
    for device in greet:
        pl.semaphore_signal(barrier, inc=1, device_id=device, device_id_type=MESH)

    @pl.when(wl == 0)
    def _():
        x[:, 0] = jnp.zeros((NQ, 16, 16, 128), F32)

    @pl.when(wl == nw - 1)
    def _():
        x[:, 2] = jnp.zeros((NQ, 16, 16, 128), F32)

    for f in range(4):
        local[f].wait()

    lane = lax.broadcasted_iota(jnp.int32, (64, 128), 1)
    to_next = jnp.zeros((64, 128), F32)
    to_prev = jnp.zeros((64, 128), F32)
    for f in range(4):
        for half in range(2):
            part = x[f, 1, pl.ds(mine, 8), 8 * half : 8 * half + 8, :].reshape(64, 128)
            at = f * 32 + 16 * half
            here = (lane >= at) & (lane < at + 16)
            to_next = jnp.where(here, pltpu.roll(part, (at - 112) % 128, 1), to_next)
            at = f * 32 + 16 * (1 - half)
            here = (lane >= at) & (lane < at + 16)
            to_prev = jnp.where(here, pltpu.roll(part, at % 128, 1) if at else part, to_prev)
    edge[0] = to_next.reshape(8, 8, 128)
    edge[1] = to_prev.reshape(8, 8, 128)

    pl.semaphore_wait(barrier, len(greet))

    edges = [
        pltpu.make_async_remote_copy(
            edge.at[k], edge_in.at[k], e_s.at[k], e_r.at[k],
            device_id=greet[k], device_id_type=MESH,
        )
        for k in range(2)
    ]
    for copy in edges:
        copy.start()

    def source(q):
        return x.at[q, 1, pl.ds(mine, 8)]

    across = [
        pltpu.make_async_remote_copy(
            source(q), x.at[q, 1, pl.ds(mine, 8)], z_s.at[q], z_r.at[q],
            device_id={"stream": o}, device_id_type=MESH,
        )
        for q in range(NQ)
    ]

    def along(q, side, layers, send, recv):
        return pltpu.make_async_remote_copy(
            x.at[q, 1, pl.ds(layers, 8)], x.at[q, 2 * side, pl.ds(layers, 8)],
            send.at[q, side], recv.at[q, side],
            device_id=greet[2 + side], device_id_type=MESH,
        )

    def to_neighbours(method, q, layers, send, recv):
        for side in range(2):
            edge_of_wall = wl < nw - 1 if side == 0 else wl > 0

            @pl.when(edge_of_wall)
            def _(side=side):
                getattr(along(q, side, layers, send, recv), method)()

    def from_neighbours(q, layers, send, recv):
        for side in range(2):
            edge_of_wall = wl > 0 if side == 0 else wl < nw - 1

            @pl.when(edge_of_wall)
            def _(side=side):
                along(q, side, layers, send, recv).wait_recv()

    order = (3, 0, 1, 2, 4)
    for q in order[:4]:
        across[q].start()
    for q in order[:4]:
        to_neighbours("start", q, mine, own_s, own_r)

    for copy in edges:
        copy.wait_recv()
    before = edge_in[0].reshape(64, 128)
    after = edge_in[1].reshape(64, 128)
    left = lane % 32 < 16
    x[4, 1, pl.ds(mine, 8), 0:8, :] = jnp.where(left, before, after).reshape(8, 8, 128)
    x[4, 1, pl.ds(mine, 8), 8:16, :] = jnp.where(
        left, pltpu.roll(before, 112, 1), pltpu.roll(after, 16, 1)
    ).reshape(8, 8, 128)
    across[4].start()
    to_neighbours("start", 4, mine, own_s, own_r)

    def forward(q):
        across[q].wait_recv()
        to_neighbours("start", q, theirs, rel_s, rel_r)

    def plane_filter(q):
        from_neighbours(q, mine, own_s, own_r)
        from_neighbours(q, theirs, rel_s, rel_r)
        parts = [x[q, half : half + 2].reshape(512, 128) for half in range(2)]
        hi, lo = zip(*[hi_lo(part) for part in parts])
        hi, lo = jnp.concatenate(hi, axis=1), jnp.concatenate(lo, axis=1)
        y = jnp.dot(
            km[...], jnp.concatenate([hi, lo, hi], axis=0), preferred_element_type=F32
        )
        for half in range(2):
            hi, lo = hi_lo(y[:, 128 * half : 128 * half + 128])
            yh[q, 256 * half : 256 * half + 256, :] = hi
            yl[q, 256 * half : 256 * half + 256, :] = lo

    forward(order[0])
    local[4].wait()
    for at in range(1, NQ):
        forward(order[at])
        plane_filter(order[at - 1])
    plane_filter(order[NQ - 1])

    local[6].wait()
    rims = jnp.zeros((512, 128), F32)
    m[:, 0] = jnp.zeros((4, 32, 128), F32)
    m[:, 17] = jnp.zeros((4, 32, 128), F32)
    for f in range(4):
        hi = jnp.concatenate([yh[f], yh[4]], axis=1)
        lo = jnp.concatenate([yl[f], yl[4]], axis=1)
        out = jnp.dot(
            jnp.concatenate([hi, lo, hi], axis=1), wm[f], preferred_element_type=F32
        )
        for half in range(2):
            m[f, 1:17, 16 * half : 16 * half + 16, :] = out[
                256 * half : 256 * half + 256, :128
            ].reshape(16, 16, 128)
        rims = rims + out[:, 128:]
    for half in range(2):
        mh[:, 16 * half : 16 * half + 16, :] = rims[256 * half : 256 * half + 256].reshape(
            16, 16, 128
        )

    @pl.when(wl == 0)
    def _():
        m[:, :, 0:8, :] = jnp.zeros((4, 18, 8, 128), F32)
        mh[:, 0:8, :] = jnp.zeros((16, 8, 128), F32)

    @pl.when(wl == nw - 1)
    def _():
        m[:, :, 24:32, :] = jnp.zeros((4, 18, 8, 128), F32)
        mh[:, 24:32, :] = jnp.zeros((16, 8, 128), F32)

    local[5].wait()

    def window(q):
        return jnp.concatenate(
            [x[q, 0, :, 8:16, :], x[q, 1], x[q, 2, :, 0:8, :]], axis=1
        ).reshape(512, 128)

    def own_plane(values):
        hi, lo = hi_lo(values)
        return jnp.dot(
            ko[...], jnp.concatenate([hi, lo, hi], axis=0), preferred_element_type=F32
        )

    def own_span(f, body, rim):
        hi, lo = hi_lo(jnp.concatenate([body, rim], axis=1))
        return jnp.dot(
            jnp.concatenate([hi, lo, hi], axis=1),
            wm[f, :, 0:128],
            preferred_element_type=F32,
        )

    scalar_x = window(3)
    first_rim = own_plane(rim_product(window(4)))
    first = [own_span(i, own_plane(window(i) * scalar_x), first_rim) for i in range(3)]

    inner = pl.ds(1 + s * 8, 8)
    means = [m[f, 1:17].reshape(512, 128) for f in range(4)]
    mean_rim = mh[...].reshape(512, 128)
    second_rim = own_plane(mean_rim)
    second = [own_span(f, own_plane(means[f]), second_rim) for f in range(4)]
    flux_rim = own_plane(rim_product(mean_rim))
    flux = [own_span(i, own_plane(means[i] * means[3]), flux_rim) for i in range(3)]

    lane = lax.broadcasted_iota(jnp.int32, (128, 128), 1)
    own_rim = mh[pl.ds(mine, 8), 8:24, :].reshape(128, 128)
    own, slopes = [], []
    for f in range(4):
        c = m[f, inner, 8:24, :].reshape(128, 128)
        up = pltpu.roll(c, 127, 1)
        up = jnp.where(lane == 127, pltpu.roll(own_rim, (127 - (f * 32 + 16)) % 128, 1), up)
        down = pltpu.roll(c, 1, 1)
        down = jnp.where(lane == 0, pltpu.roll(own_rim, (128 - (f * 32 + 15)) % 128, 1), down)
        along_wall = m[f, inner, 9:25, :] - m[f, inner, 7:23, :]
        along_stream = m[f, pl.ds(2 + s * 8, 8), 8:24, :] - m[f, pl.ds(s * 8, 8), 8:24, :]
        own.append(c)
        slopes.append(
            (
                (up - down) * 0.5,
                along_wall.reshape(128, 128) * 0.5,
                along_stream.reshape(128, 128) * 0.5,
            )
        )

    clarks, similars = [], []
    ones = jnp.ones((8, 128), F32)
    sums = [[] for _ in range(5)]
    for i in range(3):
        exact = first[i] - own[i] * own[3]
        similar = flux[i] - second[i] * second[3]
        total = slopes[i][0] * slopes[3][0] + slopes[i][1] * slopes[3][1]
        clark = clark_coef * (total + slopes[i][2] * slopes[3][2])
        clarks.append(clark)
        similars.append(similar)
        pairs = (
            (exact, clark), (exact, similar), (exact, exact), (clark, clark), (similar, similar)
        )
        for k, (a, b) in enumerate(pairs):
            sums[k].append(jnp.sum((a * b).reshape(8, 16, 128), axis=0))
    st[...] = jnp.zeros((8, 128), F32)
    for k in range(5):
        rows = jnp.concatenate(sums[k], axis=0)
        got = lax.dot_general(
            ones, rows, (((1,), (1,)), ((), ())),
            precision=lax.Precision.HIGHEST, preferred_element_type=F32,
        )
        st[k : k + 1, 0:48] = got[0:1, :]

    group = xi * 2 + s
    st_a[group] = st[...]
    sends = [
        pltpu.make_async_remote_copy(
            st, st_a.at[group], a_s.at[k], a_r.at[k],
            device_id=row_mates[k], device_id_type=MESH,
        )
        for k in range(len(row_mates))
    ]
    for copy in sends:
        copy.start()
    for copy in sends:
        copy.wait_recv()
    total = st_a[0]
    for k in range(1, 2 * ROW):
        total = total + st_a[k]
    st_t[...] = total
    st_b[zi] = total
    more = [
        pltpu.make_async_remote_copy(
            st_t, st_b.at[zi], b_s.at[k], b_r.at[k],
            device_id=col_mates[k], device_id_type=MESH,
        )
        for k in range(len(col_mates))
    ]
    for copy in more:
        copy.start()
    for copy in more:
        copy.wait_recv()
    total = st_b[0]
    for k in range(1, nz):
        total = total + st_b[k]
    total = total[:, 0:48] / cells

    power_e, power_c, power_s = total[2:3], total[3:4], total[4:5]
    clark_corr = total[0:1] / jnp.sqrt((power_e + small_eps) * (power_c + small_eps))
    similar_corr = total[1:2] / jnp.sqrt((power_e + small_eps) * (power_s + small_eps))
    for i in range(3):
        cc_out[i : i + 1, :] = clark_corr[:, 16 * i : 16 * i + 16]
        sc_out[i : i + 1, :] = similar_corr[:, 16 * i : 16 * i + 16]
    spot = lax.broadcasted_iota(jnp.int32, (48, 48), 0) == lax.broadcasted_iota(
        jnp.int32, (48, 48), 1
    )
    for power, values, out in (
        (power_c, clarks, clark_out), (power_s, similars, similar_out)
    ):
        scale = 1.0 / jnp.sqrt(power + small_eps)
        scale = jnp.sum(
            jnp.where(spot, jnp.broadcast_to(scale, (48, 48)), 0.0), axis=1, keepdims=True
        )
        for i in range(3):
            rows = jnp.broadcast_to(scale[16 * i : 16 * i + 16], (16, 128))
            out[i] = values[i].reshape(8, 16, 128) * rows[None]

    for copy in edges + across + sends + more:
        copy.wait_send()
    for q in range(NQ):
        to_neighbours("wait_send", q, mine, own_s, own_r)
        to_neighbours("wait_send", q, theirs, rel_s, rel_r)


def shards(fields):
    nz = lax.axis_size("span") // ROW
    cells = float(
        fields.shape[1] * fields.shape[3] * lax.axis_size("stream") * lax.axis_size("span")
    )
    km, ko = plane_matrices()
    wm = span_matrices()
    vmem = pl.BlockSpec(memory_space=pltpu.VMEM)
    hbm = pl.BlockSpec(memory_space=pl.ANY)
    dma = pltpu.SemaphoreType.DMA

    def body(*refs):
        kernel(cells, *refs)

    return pl.pallas_call(
        body,
        out_shape=(
            jax.ShapeDtypeStruct((3, 8, 16, 128), F32),
            jax.ShapeDtypeStruct((3, 8, 16, 128), F32),
            jax.ShapeDtypeStruct((3, 16), F32),
            jax.ShapeDtypeStruct((3, 16), F32),
        ),
        in_specs=[hbm] * 4,
        out_specs=(vmem, vmem, vmem, vmem),
        scratch_shapes=[
            pltpu.VMEM((NQ, 3, 16, 16, 128), F32),
            pltpu.VMEM((2, 8, 8, 128), F32),
            pltpu.VMEM((2, 8, 8, 128), F32),
            pltpu.VMEM((256, 1536), BF),
            pltpu.VMEM((128, 1536), BF),
            pltpu.VMEM((4, 768, 256), BF),
            pltpu.VMEM((NQ, 512, 128), BF),
            pltpu.VMEM((NQ, 512, 128), BF),
            pltpu.VMEM((4, 18, 32, 128), F32),
            pltpu.VMEM((16, 32, 128), F32),
            pltpu.VMEM((8, 128), F32),
            pltpu.VMEM((8, 128), F32),
            pltpu.VMEM((2 * ROW, 8, 128), F32),
            pltpu.VMEM((8, 128), F32),
            pltpu.VMEM((nz, 8, 128), F32),
            dma((7,)),
            dma((NQ,)), dma((NQ,)),
            dma((NQ, 2)), dma((NQ, 2)),
            dma((NQ, 2)), dma((NQ, 2)),
            dma((2,)), dma((2,)),
            dma((2 * ROW - 1,)), dma((2 * ROW - 1,)),
            dma((max(nz - 1, 1),)), dma((max(nz - 1, 1),)),
        ],
        compiler_params=pltpu.CompilerParams(
            collective_id=0, has_side_effects=True, vmem_limit_bytes=48 * 2**20
        ),
        cost_estimate=pl.CostEstimate(
            flops=8_000_000_000, bytes_accessed=4_000_000, transcendentals=0
        ),
    )(fields, jnp.asarray(km), jnp.asarray(ko), jnp.asarray(wm))


def solution(mesh):
    return jax.shard_map(
        shards,
        mesh=mesh,
        in_specs=(P(None, "stream", "wall", "span"),),
        out_specs=(
            P(None, "stream", "wall", "span"),
            P(None, "stream", "wall", "span"),
            P(None, "wall"),
            P(None, "wall"),
        ),
        check_vma=False,
    )
```

```python
import math

import jax
import jax.numpy as jnp
import ml_dtypes
import numpy as np
from jax import lax
from jax.experimental import pallas as pl
from jax.experimental.pallas import tpu as pltpu
from jax.sharding import PartitionSpec as P

raw_taps = [math.exp(-((k - 8) ** 2) / 18.0) for k in range(17)]
filter_taps = [value / sum(raw_taps) for value in raw_taps]
clark_coef = 9.0
small_eps = 1e-06

MESH = pl.DeviceIdType.MESH
BF = jnp.bfloat16
F32 = jnp.float32
ROW = 4
NQ = 5


def tap(out_at, in_at):
    offset = in_at - out_at + 8
    inside = (offset >= 0) & (offset <= 16)
    return np.where(inside, np.array(filter_taps)[np.clip(offset, 0, 16)], 0.0)


def split(matrix):
    full = matrix.astype(np.float32)
    hi = full.astype(ml_dtypes.bfloat16)
    lo = (full - hi.astype(np.float32)).astype(ml_dtypes.bfloat16)
    return hi, lo


def left_stack(matrix):
    hi, lo = split(matrix)
    return np.concatenate([hi, hi, lo], axis=1)


def right_stack(matrix):
    hi, lo = split(matrix)
    return np.concatenate([hi, hi, lo], axis=0)


def plane_matrices():
    s_out, w_out = np.meshgrid(np.arange(16), np.arange(16), indexing="ij")
    s_out, w_out = s_out.reshape(-1, 1), w_out.reshape(-1, 1)
    b, s, w = np.meshgrid(np.arange(2), np.arange(16), np.arange(16), indexing="ij")
    blocks = tap(s_out, s.reshape(1, -1)) * tap(w_out + 8, (b * 16 + w).reshape(1, -1))
    s, w = np.meshgrid(np.arange(16), np.arange(32), indexing="ij")
    rows = tap(s_out, s.reshape(1, -1)) * tap(w_out + 8, w.reshape(1, -1))
    own = np.stack([left_stack(rows[:128]), left_stack(rows[128:])])
    return left_stack(blocks), own


def span_matrices():
    lane = np.arange(128)
    group, inner = lane // 32, lane % 32
    place = np.where(inner < 16, inner - 16, inner + 112)
    kept = (inner >= 8) & (inner < 24)
    main = tap(lane[None, :], lane[:, None])
    result = []
    for f in range(4):
        from_rim = tap(lane[None, :], place[:, None]) * (group == f)[:, None]
        to_rim = tap(place[None, :], lane[:, None]) * ((group == f) & kept)[None, :]
        rim = tap(place[None, :], place[:, None]) * (group[:, None] == group[None, :])
        rim = rim * kept[None, :] * (1.0 if f == 0 else 0.0)
        result.append(right_stack(np.block([[main, to_rim], [from_rim, rim]])))
    return np.stack(result)


def hi_lo(values):
    hi = values.astype(BF)
    return hi, (values - hi.astype(F32)).astype(BF)


def rim_product(rims):
    lane = lax.broadcasted_iota(jnp.int32, rims.shape, 1)
    last = jnp.where(lane >= 96, rims, 0.0)
    last = last + pltpu.roll(last, 32, 1)
    last = last + pltpu.roll(last, 64, 1)
    return rims * last


def kernel(
    fields, km_in, ko_in, w_in,
    clark_out, similar_out, sums_out,
    x, edge, edge_in, km, ko, wm, yh, yl, m, mh, st, st_a, st_t, st_b,
    loc, z_s, z_r, own_s, own_r, rel_s, rel_r, e_s, e_r, a_s, a_r, b_s, b_r,
):
    p, wl, s = lax.axis_index("span"), lax.axis_index("wall"), lax.axis_index("stream")
    np_, nw = lax.axis_size("span"), lax.axis_size("wall")
    nz = np_ // ROW
    xi, zi = p % ROW, p // ROW
    o = 1 - s
    mine = pl.multiple_of(s * 8, 8)
    theirs = pl.multiple_of(o * 8, 8)

    greet = [{"span": (p + 1) % np_}, {"span": (p + np_ - 1) % np_}]
    greet += [{"wall": (wl + 1) % nw}, {"wall": (wl + nw - 1) % nw}]
    row_mates = [
        {"span": zi * ROW + (xi + k // 2) % ROW, "stream": (s + k % 2) % 2}
        for k in range(1, 2 * ROW)
    ]
    col_mates = [{"span": ((zi + k) % nz) * ROW + xi} for k in range(1, nz)]
    greet += row_mates + col_mates

    local = [
        pltpu.make_async_copy(fields.at[f], x.at[f, 1, pl.ds(mine, 8)], loc.at[f])
        for f in range(4)
    ]
    local += [
        pltpu.make_async_copy(km_in, km, loc.at[4]),
        pltpu.make_async_copy(ko_in.at[s], ko, loc.at[5]),
        pltpu.make_async_copy(w_in, wm, loc.at[6]),
    ]
    for copy in local:
        copy.start()

    barrier = pltpu.get_barrier_semaphore()
    for device in greet:
        pl.semaphore_signal(barrier, inc=1, device_id=device, device_id_type=MESH)

    @pl.when(wl == 0)
    def _():
        x[:, 0] = jnp.zeros((NQ, 16, 16, 128), F32)

    @pl.when(wl == nw - 1)
    def _():
        x[:, 2] = jnp.zeros((NQ, 16, 16, 128), F32)

    for f in range(4):
        local[f].wait()

    lane = lax.broadcasted_iota(jnp.int32, (64, 128), 1)
    to_next = jnp.zeros((64, 128), F32)
    to_prev = jnp.zeros((64, 128), F32)
    for f in range(4):
        for half in range(2):
            part = x[f, 1, pl.ds(mine, 8), 8 * half : 8 * half + 8, :].reshape(64, 128)
            at = f * 32 + 16 * half
            here = (lane >= at) & (lane < at + 16)
            to_next = jnp.where(here, pltpu.roll(part, (at - 112) % 128, 1), to_next)
            at = f * 32 + 16 * (1 - half)
            here = (lane >= at) & (lane < at + 16)
            to_prev = jnp.where(here, pltpu.roll(part, at % 128, 1) if at else part, to_prev)
    edge[0] = to_next.reshape(8, 8, 128)
    edge[1] = to_prev.reshape(8, 8, 128)

    pl.semaphore_wait(barrier, len(greet))

    edges = [
        pltpu.make_async_remote_copy(
            edge.at[k], edge_in.at[k], e_s.at[k], e_r.at[k],
            device_id=greet[k], device_id_type=MESH,
        )
        for k in range(2)
    ]
    for copy in edges:
        copy.start()

    def source(q):
        return x.at[q, 1, pl.ds(mine, 8)]

    across = [
        pltpu.make_async_remote_copy(
            source(q), x.at[q, 1, pl.ds(mine, 8)], z_s.at[q], z_r.at[q],
            device_id={"stream": o}, device_id_type=MESH,
        )
        for q in range(NQ)
    ]

    def along(q, side, layers, send, recv):
        return pltpu.make_async_remote_copy(
            x.at[q, 1, pl.ds(layers, 8)], x.at[q, 2 * side, pl.ds(layers, 8)],
            send.at[q, side], recv.at[q, side],
            device_id=greet[2 + side], device_id_type=MESH,
        )

    def to_neighbours(method, q, layers, send, recv):
        for side in range(2):
            edge_of_wall = wl < nw - 1 if side == 0 else wl > 0

            @pl.when(edge_of_wall)
            def _(side=side):
                getattr(along(q, side, layers, send, recv), method)()

    def from_neighbours(q, layers, send, recv):
        for side in range(2):
            edge_of_wall = wl > 0 if side == 0 else wl < nw - 1

            @pl.when(edge_of_wall)
            def _(side=side):
                along(q, side, layers, send, recv).wait_recv()

    order = (3, 0, 1, 2, 4)
    for q in order[:4]:
        across[q].start()
    for q in order[:4]:
        to_neighbours("start", q, mine, own_s, own_r)

    for copy in edges:
        copy.wait_recv()
    before = edge_in[0].reshape(64, 128)
    after = edge_in[1].reshape(64, 128)
    left = lane % 32 < 16
    x[4, 1, pl.ds(mine, 8), 0:8, :] = jnp.where(left, before, after).reshape(8, 8, 128)
    x[4, 1, pl.ds(mine, 8), 8:16, :] = jnp.where(
        left, pltpu.roll(before, 112, 1), pltpu.roll(after, 16, 1)
    ).reshape(8, 8, 128)
    across[4].start()
    to_neighbours("start", 4, mine, own_s, own_r)

    def forward(q):
        across[q].wait_recv()
        to_neighbours("start", q, theirs, rel_s, rel_r)

    def plane_filter(q):
        from_neighbours(q, mine, own_s, own_r)
        from_neighbours(q, theirs, rel_s, rel_r)
        parts = [x[q, half : half + 2].reshape(512, 128) for half in range(2)]
        hi, lo = zip(*[hi_lo(part) for part in parts])
        hi, lo = jnp.concatenate(hi, axis=1), jnp.concatenate(lo, axis=1)
        y = jnp.dot(
            km[...], jnp.concatenate([hi, lo, hi], axis=0), preferred_element_type=F32
        )
        for half in range(2):
            hi, lo = hi_lo(y[:, 128 * half : 128 * half + 128])
            yh[q, 256 * half : 256 * half + 256, :] = hi
            yl[q, 256 * half : 256 * half + 256, :] = lo

    forward(order[0])
    local[4].wait()
    for at in range(1, NQ):
        forward(order[at])
        plane_filter(order[at - 1])
    plane_filter(order[NQ - 1])

    local[6].wait()
    rims = jnp.zeros((512, 128), F32)
    m[:, 0] = jnp.zeros((4, 32, 128), F32)
    m[:, 17] = jnp.zeros((4, 32, 128), F32)
    for f in range(4):
        hi = jnp.concatenate([yh[f], yh[4]], axis=1)
        lo = jnp.concatenate([yl[f], yl[4]], axis=1)
        out = jnp.dot(
            jnp.concatenate([hi, lo, hi], axis=1), wm[f], preferred_element_type=F32
        )
        for half in range(2):
            m[f, 1:17, 16 * half : 16 * half + 16, :] = out[
                256 * half : 256 * half + 256, :128
            ].reshape(16, 16, 128)
        rims = rims + out[:, 128:]
    for half in range(2):
        mh[:, 16 * half : 16 * half + 16, :] = rims[256 * half : 256 * half + 256].reshape(
            16, 16, 128
        )

    @pl.when(wl == 0)
    def _():
        m[:, :, 0:8, :] = jnp.zeros((4, 18, 8, 128), F32)
        mh[:, 0:8, :] = jnp.zeros((16, 8, 128), F32)

    @pl.when(wl == nw - 1)
    def _():
        m[:, :, 24:32, :] = jnp.zeros((4, 18, 8, 128), F32)
        mh[:, 24:32, :] = jnp.zeros((16, 8, 128), F32)

    local[5].wait()

    def window(q):
        return jnp.concatenate(
            [x[q, 0, :, 8:16, :], x[q, 1], x[q, 2, :, 0:8, :]], axis=1
        ).reshape(512, 128)

    def own_plane(values):
        hi, lo = hi_lo(values)
        return jnp.dot(
            ko[...], jnp.concatenate([hi, lo, hi], axis=0), preferred_element_type=F32
        )

    def own_span(f, body, rim):
        hi, lo = hi_lo(jnp.concatenate([body, rim], axis=1))
        return jnp.dot(
            jnp.concatenate([hi, lo, hi], axis=1),
            wm[f, :, 0:128],
            preferred_element_type=F32,
        )

    scalar_x = window(3)
    first_rim = own_plane(rim_product(window(4)))
    first = [own_span(i, own_plane(window(i) * scalar_x), first_rim) for i in range(3)]

    inner = pl.ds(1 + s * 8, 8)
    means = [m[f, 1:17].reshape(512, 128) for f in range(4)]
    mean_rim = mh[...].reshape(512, 128)
    second_rim = own_plane(mean_rim)
    second = [own_span(f, own_plane(means[f]), second_rim) for f in range(4)]
    flux_rim = own_plane(rim_product(mean_rim))
    flux = [own_span(i, own_plane(means[i] * means[3]), flux_rim) for i in range(3)]

    lane = lax.broadcasted_iota(jnp.int32, (128, 128), 1)
    own_rim = mh[pl.ds(mine, 8), 8:24, :].reshape(128, 128)
    own, slopes = [], []
    for f in range(4):
        c = m[f, inner, 8:24, :].reshape(128, 128)
        up = pltpu.roll(c, 127, 1)
        up = jnp.where(lane == 127, pltpu.roll(own_rim, (127 - (f * 32 + 16)) % 128, 1), up)
        down = pltpu.roll(c, 1, 1)
        down = jnp.where(lane == 0, pltpu.roll(own_rim, (128 - (f * 32 + 15)) % 128, 1), down)
        along_wall = m[f, inner, 9:25, :] - m[f, inner, 7:23, :]
        along_stream = m[f, pl.ds(2 + s * 8, 8), 8:24, :] - m[f, pl.ds(s * 8, 8), 8:24, :]
        own.append(c)
        slopes.append(
            (
                (up - down) * 0.5,
                along_wall.reshape(128, 128) * 0.5,
                along_stream.reshape(128, 128) * 0.5,
            )
        )

    ones = jnp.ones((8, 128), F32)
    sums = [[] for _ in range(5)]
    for i in range(3):
        exact = first[i] - own[i] * own[3]
        similar = flux[i] - second[i] * second[3]
        total = slopes[i][0] * slopes[3][0] + slopes[i][1] * slopes[3][1]
        clark = clark_coef * (total + slopes[i][2] * slopes[3][2])
        clark_out[i] = clark.reshape(8, 16, 128)
        similar_out[i] = similar.reshape(8, 16, 128)
        pairs = (
            (exact, clark), (exact, similar), (exact, exact), (clark, clark), (similar, similar)
        )
        for k, (a, b) in enumerate(pairs):
            sums[k].append(jnp.sum((a * b).reshape(8, 16, 128), axis=0))
    st[...] = jnp.zeros((8, 128), F32)
    for k in range(5):
        rows = jnp.concatenate(sums[k], axis=0)
        got = lax.dot_general(
            ones, rows, (((1,), (1,)), ((), ())),
            precision=lax.Precision.HIGHEST, preferred_element_type=F32,
        )
        st[k : k + 1, 0:48] = got[0:1, :]

    group = xi * 2 + s
    st_a[group] = st[...]
    sends = [
        pltpu.make_async_remote_copy(
            st, st_a.at[group], a_s.at[k], a_r.at[k],
            device_id=row_mates[k], device_id_type=MESH,
        )
        for k in range(len(row_mates))
    ]
    for copy in sends:
        copy.start()
    for copy in sends:
        copy.wait_recv()
    total = st_a[0]
    for k in range(1, 2 * ROW):
        total = total + st_a[k]
    st_t[...] = total
    st_b[zi] = total
    more = [
        pltpu.make_async_remote_copy(
            st_t, st_b.at[zi], b_s.at[k], b_r.at[k],
            device_id=col_mates[k], device_id_type=MESH,
        )
        for k in range(len(col_mates))
    ]
    for copy in more:
        copy.start()
    for copy in more:
        copy.wait_recv()
    total = st_b[0]
    for k in range(1, nz):
        total = total + st_b[k]
    sums_out[...] = total

    for copy in edges + across + sends + more:
        copy.wait_send()
    for q in range(NQ):
        to_neighbours("wait_send", q, mine, own_s, own_r)
        to_neighbours("wait_send", q, theirs, rel_s, rel_r)


def finish(
    cells, clark, similar, sums, clark_out, similar_out, cc_out, sc_out,
    c_buf, s_buf, cc_buf, sc_buf, sem,
):
    total = sums[:, 0:48] / cells
    power_e, power_c, power_s = total[2:3], total[3:4], total[4:5]
    clark_corr = total[0:1] / jnp.sqrt((power_e + small_eps) * (power_c + small_eps))
    similar_corr = total[1:2] / jnp.sqrt((power_e + small_eps) * (power_s + small_eps))
    copies = []

    def send(src, dst):
        copy = pltpu.make_async_copy(src, dst, sem.at[len(copies)])
        copy.start()
        copies.append(copy)

    spot = lax.broadcasted_iota(jnp.int32, (48, 48), 0) == lax.broadcasted_iota(
        jnp.int32, (48, 48), 1
    )
    for power, values, buf, out in (
        (power_c, clark, c_buf, clark_out), (power_s, similar, s_buf, similar_out)
    ):
        scale = 1.0 / jnp.sqrt(power + small_eps)
        scale = jnp.sum(
            jnp.where(spot, jnp.broadcast_to(scale, (48, 48)), 0.0), axis=1, keepdims=True
        )
        for i in range(3):
            rows = jnp.broadcast_to(scale[16 * i : 16 * i + 16], (16, 128))
            buf[i] = values[i] * rows[None]
            send(buf.at[i], out.at[i])
    for corr, buf, out in ((clark_corr, cc_buf, cc_out), (similar_corr, sc_buf, sc_out)):
        for i in range(3):
            buf[i : i + 1, :] = corr[:, 16 * i : 16 * i + 16]
        send(buf, out)
    for copy in copies:
        copy.wait()


def shards(fields):
    nz = lax.axis_size("span") // ROW
    cells = float(
        fields.shape[1] * fields.shape[3] * lax.axis_size("stream") * lax.axis_size("span")
    )
    km, ko = plane_matrices()
    wm = span_matrices()
    vmem = pl.BlockSpec(memory_space=pltpu.VMEM)
    hbm = pl.BlockSpec(memory_space=pltpu.HBM)
    dma = pltpu.SemaphoreType.DMA

    flux = jax.ShapeDtypeStruct((3, 8, 16, 128), F32)
    corr = jax.ShapeDtypeStruct((3, 16), F32)
    clark, similar, sums = pl.pallas_call(
        kernel,
        out_shape=(flux, flux, jax.ShapeDtypeStruct((8, 128), F32)),
        in_specs=[hbm] * 4,
        out_specs=(vmem, vmem, vmem),
        scratch_shapes=[
            pltpu.VMEM((NQ, 3, 16, 16, 128), F32),
            pltpu.VMEM((2, 8, 8, 128), F32),
            pltpu.VMEM((2, 8, 8, 128), F32),
            pltpu.VMEM((256, 1536), BF),
            pltpu.VMEM((128, 1536), BF),
            pltpu.VMEM((4, 768, 256), BF),
            pltpu.VMEM((NQ, 512, 128), BF),
            pltpu.VMEM((NQ, 512, 128), BF),
            pltpu.VMEM((4, 18, 32, 128), F32),
            pltpu.VMEM((16, 32, 128), F32),
            pltpu.VMEM((8, 128), F32),
            pltpu.VMEM((2 * ROW, 8, 128), F32),
            pltpu.VMEM((8, 128), F32),
            pltpu.VMEM((nz, 8, 128), F32),
            dma((7,)),
            dma((NQ,)), dma((NQ,)),
            dma((NQ, 2)), dma((NQ, 2)),
            dma((NQ, 2)), dma((NQ, 2)),
            dma((2,)), dma((2,)),
            dma((2 * ROW - 1,)), dma((2 * ROW - 1,)),
            dma((max(nz - 1, 1),)), dma((max(nz - 1, 1),)),
        ],
        compiler_params=pltpu.CompilerParams(
            collective_id=0, has_side_effects=True, vmem_limit_bytes=54680 * 2**10
        ),
        cost_estimate=pl.CostEstimate(
            flops=8_000_000_000, bytes_accessed=4_000_000, transcendentals=0
        ),
    )(fields, jnp.asarray(km), jnp.asarray(ko), jnp.asarray(wm))

    def last(*refs):
        finish(cells, *refs)

    return pl.pallas_call(
        last,
        out_shape=(flux, flux, corr, corr),
        in_specs=[vmem] * 3,
        out_specs=(hbm, hbm, hbm, hbm),
        scratch_shapes=[
            pltpu.VMEM((3, 8, 16, 128), F32),
            pltpu.VMEM((3, 8, 16, 128), F32),
            pltpu.VMEM((3, 16), F32),
            pltpu.VMEM((3, 16), F32),
            dma((8,)),
        ],
        compiler_params=pltpu.CompilerParams(vmem_limit_bytes=8 * 2**20),
    )(clark, similar, sums)


def solution(mesh):
    return jax.shard_map(
        shards,
        mesh=mesh,
        in_specs=(P(None, "stream", "wall", "span"),),
        out_specs=(
            P(None, "stream", "wall", "span"),
            P(None, "stream", "wall", "span"),
            P(None, "wall"),
            P(None, "wall"),
        ),
        check_vma=False,
    )
```

```python
import math

import jax
import jax.numpy as jnp
import ml_dtypes
import numpy as np
from jax import lax
from jax.experimental import pallas as pl
from jax.experimental.pallas import tpu as pltpu
from jax.sharding import PartitionSpec as P

raw_taps = [math.exp(-((k - 8) ** 2) / 18.0) for k in range(17)]
filter_taps = [value / sum(raw_taps) for value in raw_taps]
clark_coef = 9.0
small_eps = 1e-06

MESH = pl.DeviceIdType.MESH
BF = jnp.bfloat16
F32 = jnp.float32
ROW = 4
NQ = 5


def tap(out_at, in_at):
    offset = in_at - out_at + 8
    inside = (offset >= 0) & (offset <= 16)
    return np.where(inside, np.array(filter_taps)[np.clip(offset, 0, 16)], 0.0)


def split(matrix):
    full = matrix.astype(np.float32)
    hi = full.astype(ml_dtypes.bfloat16)
    lo = (full - hi.astype(np.float32)).astype(ml_dtypes.bfloat16)
    return hi, lo


def left_stack(matrix):
    hi, lo = split(matrix)
    return np.concatenate([hi, hi, lo], axis=1)


def right_stack(matrix):
    hi, lo = split(matrix)
    return np.concatenate([hi, hi, lo], axis=0)


def plane_matrices():
    s_out, w_out = np.meshgrid(np.arange(16), np.arange(16), indexing="ij")
    s_out, w_out = s_out.reshape(-1, 1), w_out.reshape(-1, 1)
    b, s, w = np.meshgrid(np.arange(2), np.arange(16), np.arange(16), indexing="ij")
    blocks = tap(s_out, s.reshape(1, -1)) * tap(w_out + 8, (b * 16 + w).reshape(1, -1))
    s, w = np.meshgrid(np.arange(16), np.arange(32), indexing="ij")
    rows = tap(s_out, s.reshape(1, -1)) * tap(w_out + 8, w.reshape(1, -1))
    own = np.stack([left_stack(rows[:128]), left_stack(rows[128:])])
    return left_stack(blocks), own


def span_matrices():
    lane = np.arange(128)
    group, inner = lane // 32, lane % 32
    place = np.where(inner < 16, inner - 16, inner + 112)
    kept = (inner >= 8) & (inner < 24)
    main = tap(lane[None, :], lane[:, None])
    result = []
    for f in range(4):
        from_rim = tap(lane[None, :], place[:, None]) * (group == f)[:, None]
        to_rim = tap(place[None, :], lane[:, None]) * ((group == f) & kept)[None, :]
        rim = tap(place[None, :], place[:, None]) * (group == f)[:, None]
        rim = rim * ((group == f) & kept)[None, :]
        result.append(right_stack(np.block([[main, to_rim], [from_rim, rim]])))
    return np.stack(result)


def hi_lo(values):
    hi = values.astype(BF)
    return hi, (values - hi.astype(F32)).astype(BF)


def rim_product(rims):
    lane = lax.broadcasted_iota(jnp.int32, rims.shape, 1)
    last = jnp.where(lane >= 96, rims, 0.0)
    last = last + pltpu.roll(last, 32, 1)
    last = last + pltpu.roll(last, 64, 1)
    return rims * last


def kernel(
    fields, km_in, ko_in, w_in,
    clark_out, similar_out, sums_out,
    x, edge, edge_in, km, ko, wm, yh, yl, m, mh, st, st_a, st_t, st_b,
    loc, z_s, z_r, own_s, own_r, rel_s, rel_r, e_s, e_r, a_s, a_r, b_s, b_r,
):
    p, wl, s = lax.axis_index("span"), lax.axis_index("wall"), lax.axis_index("stream")
    np_, nw = lax.axis_size("span"), lax.axis_size("wall")
    nz = np_ // ROW
    xi, zi = p % ROW, p // ROW
    o = 1 - s
    mine = pl.multiple_of(s * 8, 8)
    theirs = pl.multiple_of(o * 8, 8)

    greet = [{"span": (p + 1) % np_}, {"span": (p + np_ - 1) % np_}]
    greet += [{"wall": (wl + 1) % nw}, {"wall": (wl + nw - 1) % nw}]
    row_mates = [
        {"span": zi * ROW + (xi + k // 2) % ROW, "stream": (s + k % 2) % 2}
        for k in range(1, 2 * ROW)
    ]
    col_mates = [{"span": ((zi + k) % nz) * ROW + xi} for k in range(1, nz)]
    greet += row_mates + col_mates

    local = [
        pltpu.make_async_copy(fields.at[f], x.at[f, 1, pl.ds(mine, 8)], loc.at[f])
        for f in range(4)
    ]
    local += [
        pltpu.make_async_copy(km_in, km, loc.at[4]),
        pltpu.make_async_copy(ko_in.at[s], ko, loc.at[5]),
        pltpu.make_async_copy(w_in, wm, loc.at[6]),
    ]
    for copy in local:
        copy.start()

    barrier = pltpu.get_barrier_semaphore()
    for device in greet:
        pl.semaphore_signal(barrier, inc=1, device_id=device, device_id_type=MESH)

    @pl.when(wl == 0)
    def _():
        x[:, 0] = jnp.zeros((NQ, 16, 16, 128), F32)

    @pl.when(wl == nw - 1)
    def _():
        x[:, 2] = jnp.zeros((NQ, 16, 16, 128), F32)

    for f in range(4):
        local[f].wait()

    lane = lax.broadcasted_iota(jnp.int32, (64, 128), 1)
    to_next = jnp.zeros((64, 128), F32)
    to_prev = jnp.zeros((64, 128), F32)
    for f in range(4):
        for half in range(2):
            part = x[f, 1, pl.ds(mine, 8), 8 * half : 8 * half + 8, :].reshape(64, 128)
            at = f * 32 + 16 * half
            here = (lane >= at) & (lane < at + 16)
            to_next = jnp.where(here, pltpu.roll(part, (at - 112) % 128, 1), to_next)
            at = f * 32 + 16 * (1 - half)
            here = (lane >= at) & (lane < at + 16)
            to_prev = jnp.where(here, pltpu.roll(part, at % 128, 1) if at else part, to_prev)
    edge[0] = to_next.reshape(8, 8, 128)
    edge[1] = to_prev.reshape(8, 8, 128)

    pl.semaphore_wait(barrier, len(greet))

    edges = [
        pltpu.make_async_remote_copy(
            edge.at[k], edge_in.at[k], e_s.at[k], e_r.at[k],
            device_id=greet[k], device_id_type=MESH,
        )
        for k in range(2)
    ]
    for copy in edges:
        copy.start()

    def source(q):
        return x.at[q, 1, pl.ds(mine, 8)]

    across = [
        pltpu.make_async_remote_copy(
            source(q), x.at[q, 1, pl.ds(mine, 8)], z_s.at[q], z_r.at[q],
            device_id={"stream": o}, device_id_type=MESH,
        )
        for q in range(NQ)
    ]

    def along(q, side, layers, send, recv):
        return pltpu.make_async_remote_copy(
            x.at[q, 1, pl.ds(layers, 8)], x.at[q, 2 * side, pl.ds(layers, 8)],
            send.at[q, side], recv.at[q, side],
            device_id=greet[2 + side], device_id_type=MESH,
        )

    def to_neighbours(method, q, layers, send, recv):
        for side in range(2):
            edge_of_wall = wl < nw - 1 if side == 0 else wl > 0

            @pl.when(edge_of_wall)
            def _(side=side):
                getattr(along(q, side, layers, send, recv), method)()

    def from_neighbours(q, layers, send, recv):
        for side in range(2):
            edge_of_wall = wl > 0 if side == 0 else wl < nw - 1

            @pl.when(edge_of_wall)
            def _(side=side):
                along(q, side, layers, send, recv).wait_recv()

    def send_own(q):
        across[q].start()
        to_neighbours("start", q, mine, own_s, own_r)

    def forward(q):
        across[q].wait_recv()
        to_neighbours("start", q, theirs, rel_s, rel_r)

    def plane_filter(q):
        from_neighbours(q, mine, own_s, own_r)
        from_neighbours(q, theirs, rel_s, rel_r)
        blocks = [hi_lo(x[q, b].reshape(256, 128)) for b in range(3)]

        def pair(k):
            return jnp.concatenate(
                [
                    jnp.concatenate([blocks[0][k], blocks[1][k]], axis=0),
                    jnp.concatenate([blocks[1][k], blocks[2][k]], axis=0),
                ],
                axis=1,
            )

        hi, lo = pair(0), pair(1)
        y = jnp.dot(
            km[...], jnp.concatenate([hi, lo, hi], axis=0), preferred_element_type=F32
        )
        for half in range(2):
            hi, lo = hi_lo(y[:, 128 * half : 128 * half + 128])
            yh[q, 256 * half : 256 * half + 256, :] = hi
            yl[q, 256 * half : 256 * half + 256, :] = lo

    low = jnp.where(wl > 0, 1.0, 0.0)
    high = jnp.where(wl < nw - 1, 1.0, 0.0)

    def mean_field(f):
        hi = jnp.concatenate([yh[f], yh[4]], axis=1)
        lo = jnp.concatenate([yl[f], yl[4]], axis=1)
        out = jnp.dot(
            jnp.concatenate([hi, lo, hi], axis=1), wm[f], preferred_element_type=F32
        ).reshape(2, 16, 16, 256)
        parts = (out[0, :, 0:8] * low, out[0, :, 8:16], out[1, :, 0:8], out[1, :, 8:16] * high)
        for k in range(4):
            m[f, 1:17, 8 * k : 8 * k + 8, :] = parts[k][:, :, :128]
            mh[f, :, 8 * k : 8 * k + 8, :] = parts[k][:, :, 128:]

    def window(q):
        return jnp.concatenate(
            [x[q, 0, :, 8:16, :], x[q, 1], x[q, 2, :, 0:8, :]], axis=1
        ).reshape(512, 128)

    def own_plane(values):
        hi, lo = hi_lo(jnp.concatenate(values, axis=1))
        out = jnp.dot(
            ko[...], jnp.concatenate([hi, lo, hi], axis=0), preferred_element_type=F32
        )
        return [out[:, 128 * k : 128 * k + 128] for k in range(len(values))]

    def own_span(f, bodies, rims):
        rows = [jnp.concatenate(pair, axis=1) for pair in zip(bodies, rims)]
        hi, lo = hi_lo(jnp.concatenate(rows, axis=0))
        out = jnp.dot(
            jnp.concatenate([hi, lo, hi], axis=1),
            wm[f, :, 0:128],
            preferred_element_type=F32,
        )
        return [out[128 * k : 128 * k + 128] for k in range(len(bodies))]

    inner = pl.ds(1 + s * 8, 8)
    wide = lax.broadcasted_iota(jnp.int32, (128, 128), 1)

    def own_mean(f):
        c = m[f, inner, 8:24, :].reshape(128, 128)
        rim = mh[f, pl.ds(mine, 8), 8:24, :].reshape(128, 128)
        up = pltpu.roll(c, 127, 1)
        up = jnp.where(wide == 127, pltpu.roll(rim, (127 - (f * 32 + 16)) % 128, 1), up)
        down = pltpu.roll(c, 1, 1)
        down = jnp.where(wide == 0, pltpu.roll(rim, (128 - (f * 32 + 15)) % 128, 1), down)
        along_wall = m[f, inner, 9:25, :] - m[f, inner, 7:23, :]
        along_stream = m[f, pl.ds(2 + s * 8, 8), 8:24, :] - m[f, pl.ds(s * 8, 8), 8:24, :]
        return c, (
            (up - down) * 0.5,
            along_wall.reshape(128, 128) * 0.5,
            along_stream.reshape(128, 128) * 0.5,
        )

    def flat_mean(f):
        return m[f, 1:17].reshape(512, 128), mh[f].reshape(512, 128)

    ones = jnp.ones((8, 128), F32)

    def component(i, first_rim, second_t, own_t, slopes_t):
        mean, rim = flat_mean(i)
        mean_t, rim_t = flat_mean(3)
        shift = (32 * i - 96) % 128
        product_rim = rim * pltpu.roll(rim_t, shift, 1)
        both = rim + pltpu.roll(product_rim, (128 - shift) % 128, 1)
        z_x, z_m, z_p, z_r = own_plane([window(i) * window(3), mean, mean * mean_t, both])
        first, second = own_span(i, [z_x, z_m], [first_rim, z_r])
        (flux,) = own_span(3, [z_p], [z_r])
        own, slopes = own_mean(i)
        exact = first - own * own_t
        similar = flux - second * second_t
        total = slopes[0] * slopes_t[0] + slopes[1] * slopes_t[1]
        clark = clark_coef * (total + slopes[2] * slopes_t[2])
        clark_out[i] = clark.reshape(8, 16, 128)
        similar_out[i] = similar.reshape(8, 16, 128)
        pairs = (
            (exact, clark), (exact, similar), (exact, exact), (clark, clark), (similar, similar)
        )
        rows = [jnp.sum((a * b).reshape(8, 16, 128), axis=0) for a, b in pairs]
        got = lax.dot_general(
            ones, jnp.concatenate(rows, axis=0), (((1,), (1,)), ((), ())),
            precision=lax.Precision.HIGHEST, preferred_element_type=F32,
        )
        st[i : i + 1, 0:80] = got[0:1, :]

    send_own(3)
    send_own(0)

    for copy in edges:
        copy.wait_recv()
    before = edge_in[0].reshape(64, 128)
    after = edge_in[1].reshape(64, 128)
    left = lane % 32 < 16
    x[4, 1, pl.ds(mine, 8), 0:8, :] = jnp.where(left, before, after).reshape(8, 8, 128)
    x[4, 1, pl.ds(mine, 8), 8:16, :] = jnp.where(
        left, pltpu.roll(before, 112, 1), pltpu.roll(after, 16, 1)
    ).reshape(8, 8, 128)
    send_own(4)
    send_own(1)
    send_own(2)

    st[...] = jnp.zeros((8, 128), F32)
    m[:, 0] = jnp.zeros((4, 32, 128), F32)
    m[:, 17] = jnp.zeros((4, 32, 128), F32)
    forward(3)
    forward(0)
    local[4].wait()
    local[5].wait()
    local[6].wait()
    forward(4)
    plane_filter(3)
    forward(1)
    plane_filter(4)
    mean_field(3)
    (first_rim,) = own_plane([rim_product(window(4))])
    z_m, z_r = own_plane(list(flat_mean(3)))
    (second_t,) = own_span(3, [z_m], [z_r])
    own_t, slopes_t = own_mean(3)
    plane_filter(0)
    forward(2)
    mean_field(0)
    component(0, first_rim, second_t, own_t, slopes_t)
    for i in (1, 2):
        plane_filter(i)
        mean_field(i)
        component(i, first_rim, second_t, own_t, slopes_t)

    group = xi * 2 + s
    st_a[group] = st[...]
    sends = [
        pltpu.make_async_remote_copy(
            st, st_a.at[group], a_s.at[k], a_r.at[k],
            device_id=row_mates[k], device_id_type=MESH,
        )
        for k in range(len(row_mates))
    ]
    for copy in sends:
        copy.start()
    for copy in sends:
        copy.wait_recv()
    total = st_a[0]
    for k in range(1, 2 * ROW):
        total = total + st_a[k]
    st_t[...] = total
    st_b[zi] = total
    more = [
        pltpu.make_async_remote_copy(
            st_t, st_b.at[zi], b_s.at[k], b_r.at[k],
            device_id=col_mates[k], device_id_type=MESH,
        )
        for k in range(len(col_mates))
    ]
    for copy in more:
        copy.start()
    for copy in more:
        copy.wait_recv()
    total = st_b[0]
    for k in range(1, nz):
        total = total + st_b[k]
    sums_out[...] = total

    for copy in edges + across + sends + more:
        copy.wait_send()
    for q in range(NQ):
        to_neighbours("wait_send", q, mine, own_s, own_r)
        to_neighbours("wait_send", q, theirs, rel_s, rel_r)


def finish(
    cells, clark, similar, sums, clark_out, similar_out, cc_out, sc_out,
    c_buf, s_buf, cc_buf, sc_buf, sem,
):
    total = sums[0:3, 0:80] / cells
    power_e, power_c, power_s = total[:, 32:48], total[:, 48:64], total[:, 64:80]
    copies = []

    def send(src, dst):
        copy = pltpu.make_async_copy(src, dst, sem.at[len(copies)])
        copy.start()
        copies.append(copy)

    spot = lax.broadcasted_iota(jnp.int32, (16, 16), 0) == lax.broadcasted_iota(
        jnp.int32, (16, 16), 1
    )
    for power, values, buf, out in (
        (power_c, clark, c_buf, clark_out), (power_s, similar, s_buf, similar_out)
    ):
        scale = 1.0 / jnp.sqrt(power + small_eps)
        for i in range(3):
            rows = jnp.where(spot, jnp.broadcast_to(scale[i : i + 1], (16, 16)), 0.0)
            rows = jnp.broadcast_to(jnp.sum(rows, axis=1, keepdims=True), (16, 128))
            buf[i] = values[i] * rows[None]
            send(buf.at[i], out.at[i])
    cc_buf[...] = total[:, 0:16] / jnp.sqrt((power_e + small_eps) * (power_c + small_eps))
    send(cc_buf, cc_out)
    sc_buf[...] = total[:, 16:32] / jnp.sqrt((power_e + small_eps) * (power_s + small_eps))
    send(sc_buf, sc_out)
    for copy in copies:
        copy.wait()


def shards(fields):
    nz = lax.axis_size("span") // ROW
    cells = float(
        fields.shape[1] * fields.shape[3] * lax.axis_size("stream") * lax.axis_size("span")
    )
    km, ko = plane_matrices()
    wm = span_matrices()
    vmem = pl.BlockSpec(memory_space=pltpu.VMEM)
    hbm = pl.BlockSpec(memory_space=pltpu.HBM)
    dma = pltpu.SemaphoreType.DMA

    flux = jax.ShapeDtypeStruct((3, 8, 16, 128), F32)
    corr = jax.ShapeDtypeStruct((3, 16), F32)
    clark, similar, sums = pl.pallas_call(
        kernel,
        out_shape=(flux, flux, jax.ShapeDtypeStruct((8, 128), F32)),
        in_specs=[hbm] * 4,
        out_specs=(vmem, vmem, vmem),
        scratch_shapes=[
            pltpu.VMEM((NQ, 3, 16, 16, 128), F32),
            pltpu.VMEM((2, 8, 8, 128), F32),
            pltpu.VMEM((2, 8, 8, 128), F32),
            pltpu.VMEM((256, 1536), BF),
            pltpu.VMEM((128, 1536), BF),
            pltpu.VMEM((4, 768, 256), BF),
            pltpu.VMEM((NQ, 512, 128), BF),
            pltpu.VMEM((NQ, 512, 128), BF),
            pltpu.VMEM((4, 18, 32, 128), F32),
            pltpu.VMEM((4, 16, 32, 128), F32),
            pltpu.VMEM((8, 128), F32),
            pltpu.VMEM((2 * ROW, 8, 128), F32),
            pltpu.VMEM((8, 128), F32),
            pltpu.VMEM((nz, 8, 128), F32),
            dma((7,)),
            dma((NQ,)), dma((NQ,)),
            dma((NQ, 2)), dma((NQ, 2)),
            dma((NQ, 2)), dma((NQ, 2)),
            dma((2,)), dma((2,)),
            dma((2 * ROW - 1,)), dma((2 * ROW - 1,)),
            dma((max(nz - 1, 1),)), dma((max(nz - 1, 1),)),
        ],
        compiler_params=pltpu.CompilerParams(
            collective_id=0, has_side_effects=True, vmem_limit_bytes=54680 * 2**10
        ),
        cost_estimate=pl.CostEstimate(
            flops=8_000_000_000, bytes_accessed=4_000_000, transcendentals=0
        ),
    )(fields, jnp.asarray(km), jnp.asarray(ko), jnp.asarray(wm))

    def last(*refs):
        finish(cells, *refs)

    return pl.pallas_call(
        last,
        out_shape=(flux, flux, corr, corr),
        in_specs=[vmem] * 3,
        out_specs=(hbm, hbm, hbm, hbm),
        scratch_shapes=[
            pltpu.VMEM((3, 8, 16, 128), F32),
            pltpu.VMEM((3, 8, 16, 128), F32),
            pltpu.VMEM((3, 16), F32),
            pltpu.VMEM((3, 16), F32),
            dma((8,)),
        ],
        compiler_params=pltpu.CompilerParams(vmem_limit_bytes=8 * 2**20),
    )(clark, similar, sums)


def solution(mesh):
    return jax.shard_map(
        shards,
        mesh=mesh,
        in_specs=(P(None, "stream", "wall", "span"),),
        out_specs=(
            P(None, "stream", "wall", "span"),
            P(None, "stream", "wall", "span"),
            P(None, "wall"),
            P(None, "wall"),
        ),
        check_vma=False,
    )
```

```python
import math

import jax
import jax.numpy as jnp
import ml_dtypes
import numpy as np
from jax import lax
from jax.experimental import pallas as pl
from jax.experimental.pallas import tpu as pltpu
from jax.sharding import PartitionSpec as P

raw_taps = [math.exp(-((k - 8) ** 2) / 18.0) for k in range(17)]
filter_taps = [value / sum(raw_taps) for value in raw_taps]
clark_coef = 9.0
small_eps = 1e-06

MESH = pl.DeviceIdType.MESH
BF = jnp.bfloat16
F32 = jnp.float32
ROW = 4
NQ = 5


def tap(out_at, in_at):
    offset = in_at - out_at + 8
    inside = (offset >= 0) & (offset <= 16)
    return np.where(inside, np.array(filter_taps)[np.clip(offset, 0, 16)], 0.0)


def split(matrix):
    full = matrix.astype(np.float32)
    hi = full.astype(ml_dtypes.bfloat16)
    lo = (full - hi.astype(np.float32)).astype(ml_dtypes.bfloat16)
    return hi, lo


def left_stack(matrix):
    hi, lo = split(matrix)
    return np.concatenate([hi, hi, lo], axis=1)


def plane_matrices():
    near, w_out = np.meshgrid(np.arange(8), np.arange(16), indexing="ij")
    near, w_out = near.reshape(-1, 1), w_out.reshape(-1, 1)
    b, s, w = np.meshgrid(np.arange(2), np.arange(8), np.arange(16), indexing="ij")
    wall = tap(w_out + 8, (b * 16 + w).reshape(1, -1)) * 0.5
    direct, mirror = tap(near, s.reshape(1, -1)), tap(near, 15 - s.reshape(1, -1))
    folded = np.stack([left_stack((direct + mirror) * wall), left_stack((direct - mirror) * wall)])
    s_out, w_out = np.meshgrid(np.arange(16), np.arange(16), indexing="ij")
    s_out, w_out = s_out.reshape(-1, 1), w_out.reshape(-1, 1)
    s, w = np.meshgrid(np.arange(16), np.arange(32), indexing="ij")
    rows = tap(s_out, s.reshape(1, -1)) * tap(w_out + 8, w.reshape(1, -1))
    own = np.stack([left_stack(rows[:128]), left_stack(rows[128:])])
    return folded, own


def span_matrices():
    lane = np.arange(128)
    group, inner = lane // 32, lane % 32
    place = np.where(inner < 16, inner - 16, inner + 112)
    kept = (inner >= 8) & (inner < 24)
    result = []
    for f in range(4):
        columns = np.concatenate([lane, place])
        used = np.concatenate([lane >= 0, (group == f) & kept])
        cells = tap(columns[None, :], lane[:, None]) * used[None, :]
        rims = tap(columns[None, :], place[:32, None]) * used[None, :]
        (cell_hi, cell_lo), (rim_hi, rim_lo) = split(cells), split(rims)
        packed = np.zeros((128, 256), ml_dtypes.bfloat16)
        for k, part in enumerate((rim_hi, rim_hi, rim_lo)):
            at = 32 * ((f + k) % 4)
            packed[at : at + 32] = part
        result.append(np.concatenate([cell_hi, cell_hi, cell_lo, packed]))
    return np.stack(result)


def hi_lo(values):
    hi = values.astype(BF)
    return hi, (values - hi.astype(F32)).astype(BF)


def pack_rims(rims):
    hi = rims.astype(BF).astype(F32)
    group = lax.broadcasted_iota(jnp.int32, rims.shape, 1) // 32
    low, again = pltpu.roll(rims - hi, 32, 1), pltpu.roll(hi, 64, 1)

    def of_field(f):
        packed = jnp.where(group == f, hi, jnp.where(group == (f + 1) % 4, low, again))
        return packed.astype(BF)

    return of_field


def rim_product(rims):
    lane = lax.broadcasted_iota(jnp.int32, rims.shape, 1)
    last = jnp.where(lane >= 96, rims, 0.0)
    last = last + pltpu.roll(last, 32, 1)
    last = last + pltpu.roll(last, 64, 1)
    return rims * last


def kernel(
    fields, km_in, ko_in, w_in,
    clark_out, similar_out, sums_out,
    x, edge, edge_in, km, ko, wm, yh, yl, ys, m, mh, st, st_in,
    loc, z_s, z_r, y_s, y_r, e_s, e_r, a_s, a_r,
):
    p, wl, s = lax.axis_index("span"), lax.axis_index("wall"), lax.axis_index("stream")
    np_, nw = lax.axis_size("span"), lax.axis_size("wall")
    nz = np_ // ROW
    xi, zi = p % ROW, p // ROW
    o = 1 - s
    mine = pl.multiple_of(s * 8, 8)
    theirs = pl.multiple_of(o * 8, 8)

    mates = [
        {"span": ((zi + k // 8) % nz) * ROW + (xi + k % 8 // 2) % ROW, "stream": (s + k % 2) % 2}
        for k in sorted(range(1, 8 * nz), key=lambda k: -min(k // 8, nz - k // 8))
    ]
    ahead, behind = {"span": (p + 1) % np_}, {"span": (p + np_ - 1) % np_}
    above, below = {"wall": (wl + 1) % nw}, {"wall": (wl + nw - 1) % nw}
    greet = mates + [above, below]

    barrier = pltpu.get_barrier_semaphore()
    for device in greet:
        pl.semaphore_signal(barrier, inc=1, device_id=device, device_id_type=MESH)

    local = [
        pltpu.make_async_copy(fields, x.at[0:4, 1, pl.ds(mine, 8)], loc.at[0]),
        pltpu.make_async_copy(km_in, km, loc.at[1]),
        pltpu.make_async_copy(ko_in.at[s], ko, loc.at[2]),
        pltpu.make_async_copy(w_in, wm, loc.at[3]),
    ]
    for copy in local:
        copy.start()

    @pl.when(wl == 0)
    def _():
        x[:, 0] = jnp.zeros((NQ, 16, 16, 128), F32)

    @pl.when(wl == nw - 1)
    def _():
        x[:, 2] = jnp.zeros((NQ, 16, 16, 128), F32)

    local[0].wait()

    lane = lax.broadcasted_iota(jnp.int32, (64, 128), 1)
    to_next = jnp.zeros((64, 128), F32)
    to_prev = jnp.zeros((64, 128), F32)
    for f in range(4):
        for half in range(2):
            part = x[f, 1, pl.ds(mine, 8), 8 * half : 8 * half + 8, :].reshape(64, 128)
            at = f * 32 + 16 * half
            here = (lane >= at) & (lane < at + 16)
            to_next = jnp.where(here, pltpu.roll(part, (at - 112) % 128, 1), to_next)
            at = f * 32 + 16 * (1 - half)
            here = (lane >= at) & (lane < at + 16)
            to_prev = jnp.where(here, pltpu.roll(part, at % 128, 1) if at else part, to_prev)
    edge[0] = to_next.reshape(8, 8, 128)
    edge[1] = to_prev.reshape(8, 8, 128)

    pl.semaphore_wait(barrier, len(greet))

    def remote(src, dst, send, recv, device):
        return pltpu.make_async_remote_copy(
            src, dst, send, recv, device_id=device, device_id_type=MESH
        )

    def across(q):
        own = x.at[q, 1, pl.ds(mine, 8)]
        return remote(own, own, z_s.at[0], z_r.at[q], {"stream": o})

    def along(q, side, layers):
        return remote(
            x.at[q, 1, layers], x.at[q, 2 * side, layers],
            y_s.at[side], y_r.at[q, side], (above, below)[side],
        )

    def to_neighbours(q, layers):
        for side in range(2):

            @pl.when(wl < nw - 1 if side == 0 else wl > 0)
            def _(side=side):
                along(q, side, pl.ds(layers, 8)).start()

    def from_neighbours(q):
        for side in range(2):

            @pl.when(wl > 0 if side == 0 else wl < nw - 1)
            def _(side=side):
                along(q, side, pl.ds(0, 16)).wait_recv()

    def send_own(q):
        across(q).start()
        to_neighbours(q, mine)

    def forward(q):
        across(q).wait_recv()
        to_neighbours(q, theirs)

    def plane_filter(q):
        from_neighbours(q)
        folds = ([], [])
        for b in range(3):
            near = x[q, b, 0:8]
            far = jnp.concatenate([x[q, b, 15 - k : 16 - k] for k in range(8)], axis=0)
            folds[0].append(hi_lo((near + far).reshape(128, 128)))
            folds[1].append(hi_lo((near - far).reshape(128, 128)))

        def pair(blocks, k):
            return jnp.concatenate(
                [
                    jnp.concatenate([blocks[0][k], blocks[1][k]], axis=0),
                    jnp.concatenate([blocks[1][k], blocks[2][k]], axis=0),
                ],
                axis=1,
            )

        even, odd = [
            jnp.dot(
                km[k],
                jnp.concatenate([pair(fold, 0), pair(fold, 1), pair(fold, 0)], axis=0),
                preferred_element_type=F32,
            )
            for k, fold in enumerate(folds)
        ]
        near, far = even + odd, even - odd
        for half in range(2):
            lanes = slice(128 * half, 128 * half + 128)
            y = jnp.concatenate(
                [near[:, lanes]] + [far[112 - 16 * k : 128 - 16 * k, lanes] for k in range(8)],
                axis=0,
            )
            rows = slice(256 * half, 256 * half + 256)
            if q == 4:
                of_field = pack_rims(y)
                for f in range(4):
                    ys[f, rows, :] = of_field(f)
            else:
                yh[q, rows, :], yl[q, rows, :] = hi_lo(y)

    low = jnp.where(wl > 0, 1.0, 0.0)
    high = jnp.where(wl < nw - 1, 1.0, 0.0)

    def mean_field(f):
        out = jnp.dot(
            jnp.concatenate([yh[f], yl[f], yh[f], ys[f]], axis=1),
            wm[f],
            preferred_element_type=F32,
        ).reshape(2, 16, 16, 256)
        parts = (out[0, :, 0:8] * low, out[0, :, 8:16], out[1, :, 0:8], out[1, :, 8:16] * high)
        for k in range(4):
            m[f, 1:17, 8 * k : 8 * k + 8, :] = parts[k][:, :, :128]
            mh[f, :, 8 * k : 8 * k + 8, :] = parts[k][:, :, 128:]

    def window(q):
        return jnp.concatenate(
            [x[q, 0, :, 8:16, :], x[q, 1], x[q, 2, :, 0:8, :]], axis=1
        ).reshape(512, 128)

    def own_plane(values):
        hi, lo = hi_lo(jnp.concatenate(values, axis=1))
        out = jnp.dot(
            ko[...], jnp.concatenate([hi, lo, hi], axis=0), preferred_element_type=F32
        )
        return [out[:, 128 * k : 128 * k + 128] for k in range(len(values))]

    def own_span(f, bodies, rims):
        hi, lo = hi_lo(jnp.concatenate(bodies, axis=0))
        rim = jnp.concatenate([of_field(f) for of_field in rims], axis=0)
        out = jnp.dot(
            jnp.concatenate([hi, lo, hi, rim], axis=1),
            wm[f, :, 0:128],
            preferred_element_type=F32,
        )
        return [out[128 * k : 128 * k + 128] for k in range(len(bodies))]

    inner = pl.ds(1 + s * 8, 8)
    wide = lax.broadcasted_iota(jnp.int32, (128, 128), 1)

    def own_mean(f):
        c = m[f, inner, 8:24, :].reshape(128, 128)
        rim = mh[f, pl.ds(mine, 8), 8:24, :].reshape(128, 128)
        up = pltpu.roll(c, 127, 1)
        up = jnp.where(wide == 127, pltpu.roll(rim, (127 - (f * 32 + 16)) % 128, 1), up)
        down = pltpu.roll(c, 1, 1)
        down = jnp.where(wide == 0, pltpu.roll(rim, (128 - (f * 32 + 15)) % 128, 1), down)
        along_wall = m[f, inner, 9:25, :] - m[f, inner, 7:23, :]
        along_stream = m[f, pl.ds(2 + s * 8, 8), 8:24, :] - m[f, pl.ds(s * 8, 8), 8:24, :]
        return c, (
            (up - down) * 0.5,
            along_wall.reshape(128, 128) * 0.5,
            along_stream.reshape(128, 128) * 0.5,
        )

    def flat_mean(f):
        return m[f, 1:17].reshape(512, 128), mh[f].reshape(512, 128)

    ones = jnp.ones((8, 128), F32)

    def component(i, z_x, first_rim, second_t, own_t, slopes_t):
        mean, rim = flat_mean(i)
        mean_t, rim_t = flat_mean(3)
        shift = (32 * i - 96) % 128
        product_rim = rim * pltpu.roll(rim_t, shift, 1)
        both = rim + pltpu.roll(product_rim, (128 - shift) % 128, 1)
        parts = [mean, mean * mean_t, both]
        if z_x is None:
            z_m, z_p, z_r, z_x = own_plane(parts + [window(i) * window(3)])
        else:
            z_m, z_p, z_r = own_plane(parts)
        z_r = pack_rims(z_r)
        first, second = own_span(i, [z_x, z_m], [first_rim, z_r])
        (flux,) = own_span(3, [z_p], [z_r])
        own, slopes = own_mean(i)
        exact = first - own * own_t
        similar = flux - second * second_t
        total = slopes[0] * slopes_t[0] + slopes[1] * slopes_t[1]
        clark = clark_coef * (total + slopes[2] * slopes_t[2])
        clark_out[i] = clark.reshape(8, 16, 128)
        similar_out[i] = similar.reshape(8, 16, 128)
        pairs = (
            (exact, clark), (exact, similar), (exact, exact), (clark, clark), (similar, similar)
        )
        rows = [jnp.sum((a * b).reshape(8, 16, 128), axis=0) for a, b in pairs]
        got = lax.dot_general(
            ones, jnp.concatenate(rows, axis=0), (((1,), (1,)), ((), ())),
            precision=lax.Precision.HIGHEST, preferred_element_type=F32,
        )
        st[i : i + 1, 0:80] = got[0:1, :]

    across(3).start()
    for k, device in enumerate((ahead, behind)):
        remote(edge.at[k], edge_in.at[k], e_s.at[0], e_r.at[0], device).start()
    across(0).start()
    across(1).start()
    for q in (3, 0, 1):
        to_neighbours(q, mine)

    both_edges = remote(edge, edge_in, e_s.at[0], e_r.at[0], ahead)
    both_edges.wait_recv()
    before = edge_in[0].reshape(64, 128)
    after = edge_in[1].reshape(64, 128)
    left = lane % 32 < 16
    x[4, 1, pl.ds(mine, 8), 0:8, :] = jnp.where(left, before, after).reshape(8, 8, 128)
    x[4, 1, pl.ds(mine, 8), 8:16, :] = jnp.where(
        left, pltpu.roll(before, 112, 1), pltpu.roll(after, 16, 1)
    ).reshape(8, 8, 128)
    send_own(4)
    send_own(2)

    st[...] = jnp.zeros((8, 128), F32)
    m[:, 0] = jnp.zeros((4, 32, 128), F32)
    m[:, 17] = jnp.zeros((4, 32, 128), F32)
    forward(3)
    forward(0)
    for copy in local[1:]:
        copy.wait()
    forward(1)
    plane_filter(3)
    forward(4)
    plane_filter(0)
    forward(2)
    plane_filter(1)
    z_x = own_plane([window(i) * window(3) for i in range(2)])
    plane_filter(4)
    mean_field(3)
    first_rim, body_t, rim_t = own_plane([rim_product(window(4)), *flat_mean(3)])
    first_rim = pack_rims(first_rim)
    (second_t,) = own_span(3, [body_t], [pack_rims(rim_t)])
    own_t, slopes_t = own_mean(3)
    mean_field(0)
    component(0, z_x[0], first_rim, second_t, own_t, slopes_t)
    mean_field(1)
    component(1, z_x[1], first_rim, second_t, own_t, slopes_t)
    plane_filter(2)
    mean_field(2)
    component(2, None, first_rim, second_t, own_t, slopes_t)

    place = zi * 2 * ROW + xi * 2 + s
    st_in[place] = st[...]
    for device in mates:
        remote(st.at[0:3], st_in.at[place, 0:3], a_s.at[0], a_r.at[0], device).start()
    both_edges.wait_send()
    own = x.at[:, 1, pl.ds(mine, 8)]
    remote(own, own, z_s.at[0], z_r.at[0], {"stream": o}).wait_send()
    for side in range(2):

        @pl.when(wl < nw - 1 if side == 0 else wl > 0)
        def _(side=side):
            remote(
                x.at[:, 1], x.at[:, 2 * side], y_s.at[side], y_r.at[0, side], (above, below)[side]
            ).wait_send()

    several = st_in.at[0 : len(mates), 0:3]
    all_sums = remote(several, several, a_s.at[0], a_r.at[0], mates[0])
    all_sums.wait_recv()
    total = st_in[0, 0:3]
    for k in range(1, len(mates) + 1):
        total = total + st_in[k, 0:3]
    sums_out[0:3, :] = total
    sums_out[3:8, :] = jnp.zeros((5, 128), F32)

    all_sums.wait_send()


def finish(
    cells, clark, similar, sums, clark_out, similar_out, cc_out, sc_out,
    c_buf, s_buf, cc_buf, sc_buf, sem,
):
    total = sums[0:3, 0:80] / cells
    power_e, power_c, power_s = total[:, 32:48], total[:, 48:64], total[:, 64:80]
    copies = []

    def send(src, dst):
        copy = pltpu.make_async_copy(src, dst, sem.at[len(copies)])
        copy.start()
        copies.append(copy)

    spot = lax.broadcasted_iota(jnp.int32, (16, 16), 0) == lax.broadcasted_iota(
        jnp.int32, (16, 16), 1
    )
    for power, values, buf, out in (
        (power_c, clark, c_buf, clark_out), (power_s, similar, s_buf, similar_out)
    ):
        scale = 1.0 / jnp.sqrt(power + small_eps)
        for i in range(3):
            rows = jnp.where(spot, jnp.broadcast_to(scale[i : i + 1], (16, 16)), 0.0)
            rows = jnp.broadcast_to(jnp.sum(rows, axis=1, keepdims=True), (16, 128))
            buf[i] = values[i] * rows[None]
        send(buf, out)
    cc_buf[...] = total[:, 0:16] / jnp.sqrt((power_e + small_eps) * (power_c + small_eps))
    send(cc_buf, cc_out)
    sc_buf[...] = total[:, 16:32] / jnp.sqrt((power_e + small_eps) * (power_s + small_eps))
    send(sc_buf, sc_out)
    for copy in copies:
        copy.wait()


def shards(fields):
    nz = lax.axis_size("span") // ROW
    cells = float(
        fields.shape[1] * fields.shape[3] * lax.axis_size("stream") * lax.axis_size("span")
    )
    km, ko = plane_matrices()
    wm = span_matrices()
    vmem = pl.BlockSpec(memory_space=pltpu.VMEM)
    hbm = pl.BlockSpec(memory_space=pltpu.HBM)
    dma = pltpu.SemaphoreType.DMA

    flux = jax.ShapeDtypeStruct((3, 8, 16, 128), F32)
    corr = jax.ShapeDtypeStruct((3, 16), F32)
    clark, similar, sums = pl.pallas_call(
        kernel,
        out_shape=(flux, flux, jax.ShapeDtypeStruct((8, 128), F32)),
        in_specs=[hbm] * 4,
        out_specs=(vmem, vmem, vmem),
        scratch_shapes=[
            pltpu.VMEM((NQ, 3, 16, 16, 128), F32),
            pltpu.VMEM((2, 8, 8, 128), F32),
            pltpu.VMEM((2, 8, 8, 128), F32),
            pltpu.VMEM((2, 128, 768), BF),
            pltpu.VMEM((128, 1536), BF),
            pltpu.VMEM((4, 512, 256), BF),
            pltpu.VMEM((4, 512, 128), BF),
            pltpu.VMEM((4, 512, 128), BF),
            pltpu.VMEM((4, 512, 128), BF),
            pltpu.VMEM((4, 18, 32, 128), F32),
            pltpu.VMEM((4, 16, 32, 128), F32),
            pltpu.VMEM((8, 128), F32),
            pltpu.VMEM((2 * ROW * nz, 8, 128), F32),
            dma((4,)),
            dma((1,)), dma((NQ,)),
            dma((2,)), dma((NQ, 2)),
            dma((1,)), dma((1,)),
            dma((1,)), dma((1,)),
        ],
        compiler_params=pltpu.CompilerParams(
            collective_id=0, has_side_effects=True, vmem_limit_bytes=54680 * 2**10
        ),
        cost_estimate=pl.CostEstimate(
            flops=8_000_000_000, bytes_accessed=4_000_000, transcendentals=0
        ),
    )(fields, jnp.asarray(km), jnp.asarray(ko), jnp.asarray(wm))

    def last(*refs):
        finish(cells, *refs)

    return pl.pallas_call(
        last,
        out_shape=(flux, flux, corr, corr),
        in_specs=[vmem] * 3,
        out_specs=(hbm, hbm, hbm, hbm),
        scratch_shapes=[
            pltpu.VMEM((3, 8, 16, 128), F32),
            pltpu.VMEM((3, 8, 16, 128), F32),
            pltpu.VMEM((3, 16), F32),
            pltpu.VMEM((3, 16), F32),
            dma((4,)),
        ],
        compiler_params=pltpu.CompilerParams(vmem_limit_bytes=8 * 2**20),
    )(clark, similar, sums)


def solution(mesh):
    return jax.shard_map(
        shards,
        mesh=mesh,
        in_specs=(P(None, "stream", "wall", "span"),),
        out_specs=(
            P(None, "stream", "wall", "span"),
            P(None, "stream", "wall", "span"),
            P(None, "wall"),
            P(None, "wall"),
        ),
        check_vma=False,
    )
```

```python
import math

import jax
import jax.numpy as jnp
import ml_dtypes
import numpy as np
from jax import lax
from jax.experimental import pallas as pl
from jax.experimental.pallas import tpu as pltpu
from jax.sharding import PartitionSpec as P

raw_taps = [math.exp(-((k - 8) ** 2) / 18.0) for k in range(17)]
filter_taps = [value / sum(raw_taps) for value in raw_taps]
clark_coef = 9.0
small_eps = 1e-06

MESH = pl.DeviceIdType.MESH
BF = jnp.bfloat16
F32 = jnp.float32
ROW = 4
NQ = 5


def tap(out_at, in_at):
    offset = in_at - out_at + 8
    inside = (offset >= 0) & (offset <= 16)
    return np.where(inside, np.array(filter_taps)[np.clip(offset, 0, 16)], 0.0)


def split(matrix):
    full = matrix.astype(np.float32)
    hi = full.astype(ml_dtypes.bfloat16)
    lo = (full - hi.astype(np.float32)).astype(ml_dtypes.bfloat16)
    return hi, lo


def left_stack(matrix):
    hi, lo = split(matrix)
    return np.concatenate([hi, hi, lo], axis=1)


def plane_matrices():
    near, w_out = np.meshgrid(np.arange(8), np.arange(16), indexing="ij")
    near, w_out = near.reshape(-1, 1), w_out.reshape(-1, 1)
    b, s, w = np.meshgrid(np.arange(2), np.arange(8), np.arange(16), indexing="ij")
    wall = tap(w_out + 8, (b * 16 + w).reshape(1, -1)) * 0.5
    direct, mirror = tap(near, s.reshape(1, -1)), tap(near, 15 - s.reshape(1, -1))
    folded = np.stack([left_stack((direct + mirror) * wall), left_stack((direct - mirror) * wall)])
    s_out, w_out = np.meshgrid(np.arange(16), np.arange(16), indexing="ij")
    s_out, w_out = s_out.reshape(-1, 1), w_out.reshape(-1, 1)
    s, w = np.meshgrid(np.arange(16), np.arange(32), indexing="ij")
    rows = tap(s_out, s.reshape(1, -1)) * tap(w_out + 8, w.reshape(1, -1))
    own = np.stack([left_stack(rows[:128]), left_stack(rows[128:])])
    return folded, own


def span_matrices():
    lane = np.arange(128)
    group, inner = lane // 32, lane % 32
    place = np.where(inner < 16, inner - 16, inner + 112)
    kept = (inner >= 8) & (inner < 24)
    result = []
    for f in range(4):
        columns = np.concatenate([lane, place])
        used = np.concatenate([lane >= 0, (group == f) & kept])
        cells = tap(columns[None, :], lane[:, None]) * used[None, :]
        rims = tap(columns[None, :], place[:32, None]) * used[None, :]
        (cell_hi, cell_lo), (rim_hi, rim_lo) = split(cells), split(rims)
        packed = np.zeros((128, 256), ml_dtypes.bfloat16)
        for k, part in enumerate((rim_hi, rim_hi, rim_lo)):
            at = 32 * ((f + k) % 4)
            packed[at : at + 32] = part
        result.append(np.concatenate([cell_hi, cell_hi, cell_lo, packed]))
    return np.stack(result)


def hi_lo(values):
    hi = values.astype(BF)
    return hi, (values - hi.astype(F32)).astype(BF)


def pack_rims(rims):
    hi = rims.astype(BF).astype(F32)
    group = lax.broadcasted_iota(jnp.int32, rims.shape, 1) // 32
    low, again = pltpu.roll(rims - hi, 32, 1), pltpu.roll(hi, 64, 1)

    def of_field(f):
        packed = jnp.where(group == f, hi, jnp.where(group == (f + 1) % 4, low, again))
        return packed.astype(BF)

    return of_field


def rim_product(rims):
    lane = lax.broadcasted_iota(jnp.int32, rims.shape, 1)
    last = jnp.where(lane >= 96, rims, 0.0)
    last = last + pltpu.roll(last, 32, 1)
    last = last + pltpu.roll(last, 64, 1)
    return rims * last


def kernel(
    fields, km_in, ko_in, w_in,
    clark_out, similar_out, sums_out,
    x, edge, edge_in, km, ko, wm, yh, yl, ys, m, mh, st, st_in,
    loc, z_s, z_r, y_s, y_r, e_s, e_r, a_s, a_r,
):
    p, wl, s = lax.axis_index("span"), lax.axis_index("wall"), lax.axis_index("stream")
    np_, nw = lax.axis_size("span"), lax.axis_size("wall")
    nz = np_ // ROW
    xi, zi = p % ROW, p // ROW
    o = 1 - s
    mine = pl.multiple_of(s * 8, 8)
    theirs = pl.multiple_of(o * 8, 8)

    mates = [
        {"span": ((zi + k // 8) % nz) * ROW + (xi + k % 8 // 2) % ROW, "stream": (s + k % 2) % 2}
        for k in sorted(range(1, 8 * nz), key=lambda k: -min(k // 8, nz - k // 8))
    ]
    ahead, behind = {"span": (p + 1) % np_}, {"span": (p + np_ - 1) % np_}
    above, below = {"wall": (wl + 1) % nw}, {"wall": (wl + nw - 1) % nw}
    greet = mates + [above, below]

    barrier = pltpu.get_barrier_semaphore()
    for device in greet:
        pl.semaphore_signal(barrier, inc=1, device_id=device, device_id_type=MESH)

    local = [
        pltpu.make_async_copy(fields, x.at[0:4, 1, pl.ds(mine, 8)], loc.at[0]),
        pltpu.make_async_copy(km_in, km, loc.at[1]),
        pltpu.make_async_copy(ko_in.at[s], ko, loc.at[2]),
        pltpu.make_async_copy(w_in, wm, loc.at[3]),
    ]
    for copy in local:
        copy.start()

    @pl.when(wl == 0)
    def _():
        x[:, 0] = jnp.zeros((NQ, 16, 16, 128), F32)

    @pl.when(wl == nw - 1)
    def _():
        x[:, 2] = jnp.zeros((NQ, 16, 16, 128), F32)

    local[0].wait()

    lane = lax.broadcasted_iota(jnp.int32, (64, 128), 1)
    to_next = jnp.zeros((64, 128), F32)
    to_prev = jnp.zeros((64, 128), F32)
    for f in range(4):
        for half in range(2):
            part = x[f, 1, pl.ds(mine, 8), 8 * half : 8 * half + 8, :].reshape(64, 128)
            at = f * 32 + 16 * half
            here = (lane >= at) & (lane < at + 16)
            to_next = jnp.where(here, pltpu.roll(part, (at - 112) % 128, 1), to_next)
            at = f * 32 + 16 * (1 - half)
            here = (lane >= at) & (lane < at + 16)
            to_prev = jnp.where(here, pltpu.roll(part, at % 128, 1) if at else part, to_prev)
    edge[0] = to_next.reshape(8, 8, 128)
    edge[1] = to_prev.reshape(8, 8, 128)

    pl.semaphore_wait(barrier, len(greet))

    def remote(src, dst, send, recv, device):
        return pltpu.make_async_remote_copy(
            src, dst, send, recv, device_id=device, device_id_type=MESH
        )

    def across(q):
        own = x.at[q, 1, pl.ds(mine, 8)]
        return remote(own, own, z_s.at[0], z_r.at[q], {"stream": o})

    def along(q, side, layers):
        return remote(
            x.at[q, 1, layers], x.at[q, 2 * side, layers],
            y_s.at[side], y_r.at[q, side], (above, below)[side],
        )

    def to_neighbours(q, layers):
        for side in range(2):

            @pl.when(wl < nw - 1 if side == 0 else wl > 0)
            def _(side=side):
                along(q, side, pl.ds(layers, 8)).start()

    def from_neighbours(q):
        for side in range(2):

            @pl.when(wl > 0 if side == 0 else wl < nw - 1)
            def _(side=side):
                along(q, side, pl.ds(0, 16)).wait_recv()

    def send_own(q):
        across(q).start()
        to_neighbours(q, mine)

    def forward(q):
        across(q).wait_recv()
        to_neighbours(q, theirs)

    def plane_filter(q):
        from_neighbours(q)
        folds = ([], [])
        for b in range(3):
            near = x[q, b, 0:8]
            far = jnp.concatenate([x[q, b, 15 - k : 16 - k] for k in range(8)], axis=0)
            folds[0].append(hi_lo((near + far).reshape(128, 128)))
            folds[1].append(hi_lo((near - far).reshape(128, 128)))

        def pair(blocks, k):
            return jnp.concatenate(
                [
                    jnp.concatenate([blocks[0][k], blocks[1][k]], axis=0),
                    jnp.concatenate([blocks[1][k], blocks[2][k]], axis=0),
                ],
                axis=1,
            )

        even, odd = [
            jnp.dot(
                km[k],
                jnp.concatenate([pair(fold, 0), pair(fold, 1), pair(fold, 0)], axis=0),
                preferred_element_type=F32,
            )
            for k, fold in enumerate(folds)
        ]
        near, far = even + odd, even - odd
        for half in range(2):
            lanes = slice(128 * half, 128 * half + 128)
            y = jnp.concatenate(
                [near[:, lanes]] + [far[112 - 16 * k : 128 - 16 * k, lanes] for k in range(8)],
                axis=0,
            )
            rows = slice(256 * half, 256 * half + 256)
            if q == 4:
                of_field = pack_rims(y)
                for f in range(4):
                    ys[f, rows, :] = of_field(f)
            else:
                yh[q, rows, :], yl[q, rows, :] = hi_lo(y)

    low = jnp.where(wl > 0, 1.0, 0.0)
    high = jnp.where(wl < nw - 1, 1.0, 0.0)

    def mean_field(f):
        out = jnp.dot(
            jnp.concatenate([yh[f], yl[f], yh[f], ys[f]], axis=1),
            wm[f],
            preferred_element_type=F32,
        ).reshape(2, 16, 16, 256)
        parts = (out[0, :, 0:8] * low, out[0, :, 8:16], out[1, :, 0:8], out[1, :, 8:16] * high)
        for k in range(4):
            m[f, 1:17, 8 * k : 8 * k + 8, :] = parts[k][:, :, :128]
            mh[f, :, 8 * k : 8 * k + 8, :] = parts[k][:, :, 128:]

    def window(q):
        return jnp.concatenate(
            [x[q, 0, :, 8:16, :], x[q, 1], x[q, 2, :, 0:8, :]], axis=1
        ).reshape(512, 128)

    def own_plane(values):
        hi, lo = hi_lo(jnp.concatenate(values, axis=1))
        out = jnp.dot(
            ko[...], jnp.concatenate([hi, lo, hi], axis=0), preferred_element_type=F32
        )
        return [out[:, 128 * k : 128 * k + 128] for k in range(len(values))]

    def own_span(f, bodies, rims):
        hi, lo = hi_lo(jnp.concatenate(bodies, axis=0))
        rim = jnp.concatenate([of_field(f) for of_field in rims], axis=0)
        out = jnp.dot(
            jnp.concatenate([hi, lo, hi, rim], axis=1),
            wm[f, :, 0:128],
            preferred_element_type=F32,
        )
        return [out[128 * k : 128 * k + 128] for k in range(len(bodies))]

    inner = pl.ds(1 + s * 8, 8)
    wide = lax.broadcasted_iota(jnp.int32, (128, 128), 1)

    def own_mean(f):
        c = m[f, inner, 8:24, :].reshape(128, 128)
        rim = mh[f, pl.ds(mine, 8), 8:24, :].reshape(128, 128)
        up = pltpu.roll(c, 127, 1)
        up = jnp.where(wide == 127, pltpu.roll(rim, (127 - (f * 32 + 16)) % 128, 1), up)
        down = pltpu.roll(c, 1, 1)
        down = jnp.where(wide == 0, pltpu.roll(rim, (128 - (f * 32 + 15)) % 128, 1), down)
        along_wall = m[f, inner, 9:25, :] - m[f, inner, 7:23, :]
        along_stream = m[f, pl.ds(2 + s * 8, 8), 8:24, :] - m[f, pl.ds(s * 8, 8), 8:24, :]
        return c, (
            (up - down) * 0.5,
            along_wall.reshape(128, 128) * 0.5,
            along_stream.reshape(128, 128) * 0.5,
        )

    def flat_mean(f):
        return m[f, 1:17].reshape(512, 128), mh[f].reshape(512, 128)

    ones = jnp.ones((8, 128), F32)

    def component(i, z_x, first_rim, second_t, own_t, slopes_t):
        mean, rim = flat_mean(i)
        mean_t, rim_t = flat_mean(3)
        shift = (32 * i - 96) % 128
        product_rim = rim * pltpu.roll(rim_t, shift, 1)
        both = rim + pltpu.roll(product_rim, (128 - shift) % 128, 1)
        parts = [mean, mean * mean_t, both]
        if z_x is None:
            z_m, z_p, z_r, z_x = own_plane(parts + [window(i) * window(3)])
        else:
            z_m, z_p, z_r = own_plane(parts)
        z_r = pack_rims(z_r)
        first, second = own_span(i, [z_x, z_m], [first_rim, z_r])
        (flux,) = own_span(3, [z_p], [z_r])
        own, slopes = own_mean(i)
        exact = first - own * own_t
        similar = flux - second * second_t
        total = slopes[0] * slopes_t[0] + slopes[1] * slopes_t[1]
        clark = clark_coef * (total + slopes[2] * slopes_t[2])
        clark_out[i] = clark.reshape(8, 16, 128)
        similar_out[i] = similar.reshape(8, 16, 128)
        pairs = (
            (exact, clark), (exact, similar), (exact, exact), (clark, clark), (similar, similar)
        )
        rows = [jnp.sum((a * b).reshape(8, 16, 128), axis=0) for a, b in pairs]
        got = lax.dot_general(
            ones, jnp.concatenate(rows, axis=0), (((1,), (1,)), ((), ())),
            precision=lax.Precision.HIGHEST, preferred_element_type=F32,
        )
        st[i : i + 1, 0:80] = got[0:1, :]

    for k, device in enumerate((ahead, behind)):
        remote(edge.at[k], edge_in.at[k], e_s.at[0], e_r.at[0], device).start()
    across(3).start()
    across(0).start()
    for q in (3, 0):
        to_neighbours(q, mine)

    both_edges = remote(edge, edge_in, e_s.at[0], e_r.at[0], ahead)
    both_edges.wait_recv()
    before = edge_in[0].reshape(64, 128)
    after = edge_in[1].reshape(64, 128)
    left = lane % 32 < 16
    x[4, 1, pl.ds(mine, 8), 0:8, :] = jnp.where(left, before, after).reshape(8, 8, 128)
    x[4, 1, pl.ds(mine, 8), 8:16, :] = jnp.where(
        left, pltpu.roll(before, 112, 1), pltpu.roll(after, 16, 1)
    ).reshape(8, 8, 128)
    for q in (4, 1, 2):
        send_own(q)

    st[...] = jnp.zeros((8, 128), F32)
    m[:, 0] = jnp.zeros((4, 32, 128), F32)
    m[:, 17] = jnp.zeros((4, 32, 128), F32)
    forward(3)
    forward(0)
    for copy in local[1:]:
        copy.wait()
    forward(4)
    plane_filter(3)
    forward(1)
    plane_filter(0)
    (z_x,) = own_plane([window(0) * window(3)])
    forward(2)
    plane_filter(4)
    mean_field(3)
    first_rim, body_t, rim_t = own_plane([rim_product(window(4)), *flat_mean(3)])
    first_rim = pack_rims(first_rim)
    (second_t,) = own_span(3, [body_t], [pack_rims(rim_t)])
    own_t, slopes_t = own_mean(3)
    mean_field(0)
    component(0, z_x, first_rim, second_t, own_t, slopes_t)
    for i in (1, 2):
        plane_filter(i)
        mean_field(i)
        component(i, None, first_rim, second_t, own_t, slopes_t)

    place = zi * 2 * ROW + xi * 2 + s
    st_in[place] = st[...]
    for device in mates:
        remote(st.at[0:3], st_in.at[place, 0:3], a_s.at[0], a_r.at[0], device).start()
    both_edges.wait_send()
    own = x.at[:, 1, pl.ds(mine, 8)]
    remote(own, own, z_s.at[0], z_r.at[0], {"stream": o}).wait_send()
    for side in range(2):

        @pl.when(wl < nw - 1 if side == 0 else wl > 0)
        def _(side=side):
            remote(
                x.at[:, 1], x.at[:, 2 * side], y_s.at[side], y_r.at[0, side], (above, below)[side]
            ).wait_send()

    several = st_in.at[0 : len(mates), 0:3]
    all_sums = remote(several, several, a_s.at[0], a_r.at[0], mates[0])
    all_sums.wait_recv()
    total = st_in[0, 0:3]
    for k in range(1, len(mates) + 1):
        total = total + st_in[k, 0:3]
    sums_out[0:3, :] = total
    sums_out[3:8, :] = jnp.zeros((5, 128), F32)

    all_sums.wait_send()


def finish(
    cells, clark, similar, sums, clark_out, similar_out, cc_out, sc_out,
    c_buf, s_buf, cc_buf, sc_buf, sem,
):
    total = sums[0:3, 0:80] / cells
    power_e, power_c, power_s = total[:, 32:48], total[:, 48:64], total[:, 64:80]
    copies = []

    def send(src, dst):
        copy = pltpu.make_async_copy(src, dst, sem.at[len(copies)])
        copy.start()
        copies.append(copy)

    spot = lax.broadcasted_iota(jnp.int32, (16, 16), 0) == lax.broadcasted_iota(
        jnp.int32, (16, 16), 1
    )
    for power, values, buf, out in (
        (power_c, clark, c_buf, clark_out), (power_s, similar, s_buf, similar_out)
    ):
        scale = 1.0 / jnp.sqrt(power + small_eps)
        for i in range(3):
            rows = jnp.where(spot, jnp.broadcast_to(scale[i : i + 1], (16, 16)), 0.0)
            rows = jnp.broadcast_to(jnp.sum(rows, axis=1, keepdims=True), (16, 128))
            buf[i] = values[i] * rows[None]
        send(buf, out)
    cc_buf[...] = total[:, 0:16] / jnp.sqrt((power_e + small_eps) * (power_c + small_eps))
    send(cc_buf, cc_out)
    sc_buf[...] = total[:, 16:32] / jnp.sqrt((power_e + small_eps) * (power_s + small_eps))
    send(sc_buf, sc_out)
    for copy in copies:
        copy.wait()


def shards(fields):
    nz = lax.axis_size("span") // ROW
    cells = float(
        fields.shape[1] * fields.shape[3] * lax.axis_size("stream") * lax.axis_size("span")
    )
    km, ko = plane_matrices()
    wm = span_matrices()
    vmem = pl.BlockSpec(memory_space=pltpu.VMEM)
    hbm = pl.BlockSpec(memory_space=pltpu.HBM)
    dma = pltpu.SemaphoreType.DMA

    flux = jax.ShapeDtypeStruct((3, 8, 16, 128), F32)
    corr = jax.ShapeDtypeStruct((3, 16), F32)
    clark, similar, sums = pl.pallas_call(
        kernel,
        out_shape=(flux, flux, jax.ShapeDtypeStruct((8, 128), F32)),
        in_specs=[hbm] * 4,
        out_specs=(vmem, vmem, vmem),
        scratch_shapes=[
            pltpu.VMEM((NQ, 3, 16, 16, 128), F32),
            pltpu.VMEM((2, 8, 8, 128), F32),
            pltpu.VMEM((2, 8, 8, 128), F32),
            pltpu.VMEM((2, 128, 768), BF),
            pltpu.VMEM((128, 1536), BF),
            pltpu.VMEM((4, 512, 256), BF),
            pltpu.VMEM((4, 512, 128), BF),
            pltpu.VMEM((4, 512, 128), BF),
            pltpu.VMEM((4, 512, 128), BF),
            pltpu.VMEM((4, 18, 32, 128), F32),
            pltpu.VMEM((4, 16, 32, 128), F32),
            pltpu.VMEM((8, 128), F32),
            pltpu.VMEM((2 * ROW * nz, 8, 128), F32),
            dma((4,)),
            dma((1,)), dma((NQ,)),
            dma((2,)), dma((NQ, 2)),
            dma((1,)), dma((1,)),
            dma((1,)), dma((1,)),
        ],
        compiler_params=pltpu.CompilerParams(
            collective_id=0, has_side_effects=True, vmem_limit_bytes=54680 * 2**10
        ),
        cost_estimate=pl.CostEstimate(
            flops=8_000_000_000, bytes_accessed=4_000_000, transcendentals=0
        ),
    )(fields, jnp.asarray(km), jnp.asarray(ko), jnp.asarray(wm))

    def last(*refs):
        finish(cells, *refs)

    return pl.pallas_call(
        last,
        out_shape=(flux, flux, corr, corr),
        in_specs=[vmem] * 3,
        out_specs=(hbm, hbm, hbm, hbm),
        scratch_shapes=[
            pltpu.VMEM((3, 8, 16, 128), F32),
            pltpu.VMEM((3, 8, 16, 128), F32),
            pltpu.VMEM((3, 16), F32),
            pltpu.VMEM((3, 16), F32),
            dma((4,)),
        ],
        compiler_params=pltpu.CompilerParams(vmem_limit_bytes=8 * 2**20),
    )(clark, similar, sums)


def solution(mesh):
    return jax.shard_map(
        shards,
        mesh=mesh,
        in_specs=(P(None, "stream", "wall", "span"),),
        out_specs=(
            P(None, "stream", "wall", "span"),
            P(None, "stream", "wall", "span"),
            P(None, "wall"),
            P(None, "wall"),
        ),
        check_vma=False,
    )
```

```python
import math

import jax
import jax.numpy as jnp
import ml_dtypes
import numpy as np
from jax import lax
from jax.experimental import pallas as pl
from jax.experimental.pallas import tpu as pltpu
from jax.sharding import PartitionSpec as P

raw_taps = [math.exp(-((k - 8) ** 2) / 18.0) for k in range(17)]
filter_taps = [value / sum(raw_taps) for value in raw_taps]
clark_coef = 9.0
small_eps = 1e-06

MESH = pl.DeviceIdType.MESH
BF = jnp.bfloat16
F32 = jnp.float32
ROW = 4
NQ = 5


def tap(out_at, in_at):
    offset = in_at - out_at + 8
    inside = (offset >= 0) & (offset <= 16)
    return np.where(inside, np.array(filter_taps)[np.clip(offset, 0, 16)], 0.0)


def split(matrix):
    full = matrix.astype(np.float32)
    hi = full.astype(ml_dtypes.bfloat16)
    lo = (full - hi.astype(np.float32)).astype(ml_dtypes.bfloat16)
    return hi, lo


def left_stack(matrix):
    hi, lo = split(matrix)
    return np.concatenate([hi, hi, lo], axis=1)


def plane_matrices():
    near, w_out = np.meshgrid(np.arange(8), np.arange(16), indexing="ij")
    near, w_out = near.reshape(-1, 1), w_out.reshape(-1, 1)
    b, s, w = np.meshgrid(np.arange(2), np.arange(8), np.arange(16), indexing="ij")
    wall = tap(w_out + 8, (b * 16 + w).reshape(1, -1)) * 0.5
    direct, mirror = tap(near, s.reshape(1, -1)), tap(near, 15 - s.reshape(1, -1))
    folded = np.stack([left_stack((direct + mirror) * wall), left_stack((direct - mirror) * wall)])
    s_out, w_out = np.meshgrid(np.arange(16), np.arange(16), indexing="ij")
    s_out, w_out = s_out.reshape(-1, 1), w_out.reshape(-1, 1)
    s, w = np.meshgrid(np.arange(16), np.arange(32), indexing="ij")
    rows = tap(s_out, s.reshape(1, -1)) * tap(w_out + 8, w.reshape(1, -1))
    own = np.stack([left_stack(rows[:128]), left_stack(rows[128:])])
    return folded, own


def span_matrices():
    lane = np.arange(128)
    group, inner = lane // 32, lane % 32
    place = np.where(inner < 16, inner - 16, inner + 112)
    kept = (inner >= 8) & (inner < 24)
    result = []
    for f in range(4):
        columns = np.concatenate([lane, place])
        used = np.concatenate([lane >= 0, (group == f) & kept])
        cells = tap(columns[None, :], lane[:, None]) * used[None, :]
        rims = tap(columns[None, :], place[:32, None]) * used[None, :]
        (cell_hi, cell_lo), (rim_hi, rim_lo) = split(cells), split(rims)
        packed = np.zeros((128, 256), ml_dtypes.bfloat16)
        for k, part in enumerate((rim_hi, rim_hi, rim_lo)):
            at = 32 * ((f + k) % 4)
            packed[at : at + 32] = part
        result.append(np.concatenate([cell_hi, cell_hi, cell_lo, packed]))
    return np.stack(result)


def hi_lo(values):
    hi = values.astype(BF)
    return hi, (values - hi.astype(F32)).astype(BF)


def pack_rims(rims):
    hi = rims.astype(BF).astype(F32)
    group = lax.broadcasted_iota(jnp.int32, rims.shape, 1) // 32
    low, again = pltpu.roll(rims - hi, 32, 1), pltpu.roll(hi, 64, 1)

    def of_field(f):
        packed = jnp.where(group == f, hi, jnp.where(group == (f + 1) % 4, low, again))
        return packed.astype(BF)

    return of_field


def rim_product(rims):
    lane = lax.broadcasted_iota(jnp.int32, rims.shape, 1)
    last = jnp.where(lane >= 96, rims, 0.0)
    last = last + pltpu.roll(last, 32, 1)
    last = last + pltpu.roll(last, 64, 1)
    return rims * last


def kernel(
    fields, km_in, ko_in, w_in,
    clark_out, similar_out, sums_out,
    x, edge, edge_in, km, ko, wm, yh, yl, ys, m, mh, st, st_in,
    loc, z_s, z_r, y_s, y_r, e_s, e_r, a_s, a_r,
):
    p, wl, s = lax.axis_index("span"), lax.axis_index("wall"), lax.axis_index("stream")
    np_, nw = lax.axis_size("span"), lax.axis_size("wall")
    nz = np_ // ROW
    xi, zi = p % ROW, p // ROW
    o = 1 - s
    mine = pl.multiple_of(s * 8, 8)
    theirs = pl.multiple_of(o * 8, 8)

    mates = [
        {"span": ((zi + k // 8) % nz) * ROW + (xi + k % 8 // 2) % ROW, "stream": (s + k % 2) % 2}
        for k in sorted(range(1, 8 * nz), key=lambda k: -min(k // 8, nz - k // 8))
    ]
    ahead, behind = {"span": (p + 1) % np_}, {"span": (p + np_ - 1) % np_}
    above, below = {"wall": (wl + 1) % nw}, {"wall": (wl + nw - 1) % nw}
    greet = mates + [above, below]

    barrier = pltpu.get_barrier_semaphore()
    for device in greet:
        pl.semaphore_signal(barrier, inc=1, device_id=device, device_id_type=MESH)

    local = [
        pltpu.make_async_copy(fields, x.at[0:4, 1, pl.ds(mine, 8)], loc.at[0]),
        pltpu.make_async_copy(km_in, km, loc.at[1]),
        pltpu.make_async_copy(ko_in.at[s], ko, loc.at[2]),
        pltpu.make_async_copy(w_in, wm, loc.at[3]),
    ]
    for copy in local:
        copy.start()

    @pl.when(wl == 0)
    def _():
        x[:, 0] = jnp.zeros((NQ, 16, 16, 128), F32)

    @pl.when(wl == nw - 1)
    def _():
        x[:, 2] = jnp.zeros((NQ, 16, 16, 128), F32)

    local[0].wait()

    lane = lax.broadcasted_iota(jnp.int32, (64, 128), 1)
    to_next = jnp.zeros((64, 128), F32)
    to_prev = jnp.zeros((64, 128), F32)
    for f in range(4):
        for half in range(2):
            part = x[f, 1, pl.ds(mine, 8), 8 * half : 8 * half + 8, :].reshape(64, 128)
            at = f * 32 + 16 * half
            here = (lane >= at) & (lane < at + 16)
            to_next = jnp.where(here, pltpu.roll(part, (at - 112) % 128, 1), to_next)
            at = f * 32 + 16 * (1 - half)
            here = (lane >= at) & (lane < at + 16)
            to_prev = jnp.where(here, pltpu.roll(part, at % 128, 1) if at else part, to_prev)
    edge[0] = to_next.reshape(8, 8, 128)
    edge[1] = to_prev.reshape(8, 8, 128)

    pl.semaphore_wait(barrier, len(greet))

    def remote(src, dst, send, recv, device):
        return pltpu.make_async_remote_copy(
            src, dst, send, recv, device_id=device, device_id_type=MESH
        )

    def across(q):
        own = x.at[q, 1, pl.ds(mine, 8)]
        return remote(own, own, z_s.at[0], z_r.at[q], {"stream": o})

    def along(q, side, layers):
        return remote(
            x.at[q, 1, layers], x.at[q, 2 * side, layers],
            y_s.at[side], y_r.at[q, side], (above, below)[side],
        )

    def to_neighbours(q, layers):
        for side in (1, 0):

            @pl.when(wl < nw - 1 if side == 0 else wl > 0)
            def _(side=side):
                along(q, side, pl.ds(layers, 8)).start()

    def from_neighbours(q):
        for side in range(2):

            @pl.when(wl > 0 if side == 0 else wl < nw - 1)
            def _(side=side):
                along(q, side, pl.ds(0, 16)).wait_recv()

    def send_own(q):
        across(q).start()
        to_neighbours(q, mine)

    def forward(q):
        across(q).wait_recv()
        to_neighbours(q, theirs)

    def plane_filter(q):
        folds = ([], [])
        for b in range(3):
            near = x[q, b, 0:8]
            far = jnp.concatenate([x[q, b, 15 - k : 16 - k] for k in range(8)], axis=0)
            folds[0].append(hi_lo((near + far).reshape(128, 128)))
            folds[1].append(hi_lo((near - far).reshape(128, 128)))

        def pair(blocks, k):
            return jnp.concatenate(
                [
                    jnp.concatenate([blocks[0][k], blocks[1][k]], axis=0),
                    jnp.concatenate([blocks[1][k], blocks[2][k]], axis=0),
                ],
                axis=1,
            )

        even, odd = [
            jnp.dot(
                km[k],
                jnp.concatenate([pair(fold, 0), pair(fold, 1), pair(fold, 0)], axis=0),
                preferred_element_type=F32,
            )
            for k, fold in enumerate(folds)
        ]
        near, far = even + odd, even - odd
        for half in range(2):
            lanes = slice(128 * half, 128 * half + 128)
            y = jnp.concatenate(
                [near[:, lanes]] + [far[112 - 16 * k : 128 - 16 * k, lanes] for k in range(8)],
                axis=0,
            )
            rows = slice(256 * half, 256 * half + 256)
            if q == 4:
                of_field = pack_rims(y)
                for f in range(4):
                    ys[f, rows, :] = of_field(f)
            else:
                yh[q, rows, :], yl[q, rows, :] = hi_lo(y)

    low = jnp.where(wl > 0, 1.0, 0.0)
    high = jnp.where(wl < nw - 1, 1.0, 0.0)

    def mean_field(f):
        out = jnp.dot(
            jnp.concatenate([yh[f], yl[f], yh[f], ys[f]], axis=1),
            wm[f],
            preferred_element_type=F32,
        ).reshape(2, 16, 16, 256)
        parts = (out[0, :, 0:8] * low, out[0, :, 8:16], out[1, :, 0:8], out[1, :, 8:16] * high)
        for k in range(4):
            m[f, 1:17, 8 * k : 8 * k + 8, :] = parts[k][:, :, :128]
            mh[f, :, 8 * k : 8 * k + 8, :] = parts[k][:, :, 128:]

    def window(q):
        return jnp.concatenate(
            [x[q, 0, :, 8:16, :], x[q, 1], x[q, 2, :, 0:8, :]], axis=1
        ).reshape(512, 128)

    def own_plane(values):
        hi, lo = hi_lo(jnp.concatenate(values, axis=1))
        out = jnp.dot(
            ko[...], jnp.concatenate([hi, lo, hi], axis=0), preferred_element_type=F32
        )
        return [out[:, 128 * k : 128 * k + 128] for k in range(len(values))]

    def own_span(f, bodies, rims):
        hi, lo = hi_lo(jnp.concatenate(bodies, axis=0))
        rim = jnp.concatenate([of_field(f) for of_field in rims], axis=0)
        out = jnp.dot(
            jnp.concatenate([hi, lo, hi, rim], axis=1),
            wm[f, :, 0:128],
            preferred_element_type=F32,
        )
        return [out[128 * k : 128 * k + 128] for k in range(len(bodies))]

    inner = pl.ds(1 + s * 8, 8)
    wide = lax.broadcasted_iota(jnp.int32, (128, 128), 1)

    def own_mean(f):
        c = m[f, inner, 8:24, :].reshape(128, 128)
        rim = mh[f, pl.ds(mine, 8), 8:24, :].reshape(128, 128)
        up = pltpu.roll(c, 127, 1)
        up = jnp.where(wide == 127, pltpu.roll(rim, (127 - (f * 32 + 16)) % 128, 1), up)
        down = pltpu.roll(c, 1, 1)
        down = jnp.where(wide == 0, pltpu.roll(rim, (128 - (f * 32 + 15)) % 128, 1), down)
        along_wall = m[f, inner, 9:25, :] - m[f, inner, 7:23, :]
        along_stream = m[f, pl.ds(2 + s * 8, 8), 8:24, :] - m[f, pl.ds(s * 8, 8), 8:24, :]
        return c, (
            (up - down) * 0.5,
            along_wall.reshape(128, 128) * 0.5,
            along_stream.reshape(128, 128) * 0.5,
        )

    def flat_mean(f):
        return m[f, 1:17].reshape(512, 128), mh[f].reshape(512, 128)

    ones = jnp.ones((8, 128), F32)

    def parts_of(i, place):
        mean, rim = flat_mean(i)
        mean_t, rim_t = flat_mean(3)
        product_rim = rim * pltpu.roll(rim_t, (32 * i - 96) % 128, 1)
        both = rim + pltpu.roll(product_rim, 32 * (place - i) % 128, 1)
        return [window(i) * window(3), mean, mean * mean_t, both]

    def component(i, place, planes, first_rim, second_t, own_t, slopes_t):
        z_x, z_m, z_p, z_r = planes
        z_r = pack_rims(z_r)
        first, second = own_span(i, [z_x, z_m], [first_rim, z_r])
        (flux,) = own_span(place, [z_p], [z_r])
        own, slopes = own_mean(i)
        exact = first - own * own_t
        similar = flux - second * second_t
        total = slopes[0] * slopes_t[0] + slopes[1] * slopes_t[1]
        clark = clark_coef * (total + slopes[2] * slopes_t[2])
        clark_out[i] = clark.reshape(8, 16, 128)
        similar_out[i] = similar.reshape(8, 16, 128)
        pairs = (
            (exact, clark), (exact, similar), (exact, exact), (clark, clark), (similar, similar)
        )
        rows = [jnp.sum((a * b).reshape(8, 16, 128), axis=0) for a, b in pairs]
        got = lax.dot_general(
            ones, jnp.concatenate(rows, axis=0), (((1,), (1,)), ((), ())),
            precision=lax.Precision.HIGHEST, preferred_element_type=F32,
        )
        st[i : i + 1, 0:80] = got[0:1, :]

    for k, device in enumerate((ahead, behind)):
        remote(edge.at[k], edge_in.at[k], e_s.at[0], e_r.at[0], device).start()
    across(3).start()
    across(0).start()
    for q in (3, 0):
        to_neighbours(q, mine)

    both_edges = remote(edge, edge_in, e_s.at[0], e_r.at[0], ahead)
    both_edges.wait_recv()
    before = edge_in[0].reshape(64, 128)
    after = edge_in[1].reshape(64, 128)
    left = lane % 32 < 16
    x[4, 1, pl.ds(mine, 8), 0:8, :] = jnp.where(left, before, after).reshape(8, 8, 128)
    x[4, 1, pl.ds(mine, 8), 8:16, :] = jnp.where(
        left, pltpu.roll(before, 112, 1), pltpu.roll(after, 16, 1)
    ).reshape(8, 8, 128)
    for q in (4, 1, 2):
        send_own(q)

    st[...] = jnp.zeros((8, 128), F32)
    m[:, 0] = jnp.zeros((4, 32, 128), F32)
    m[:, 17] = jnp.zeros((4, 32, 128), F32)
    forward(3)
    forward(0)
    for copy in local[1:]:
        copy.wait()
    forward(4)
    from_neighbours(3)
    plane_filter(3)
    forward(1)
    from_neighbours(0)
    plane_filter(0)
    forward(2)
    from_neighbours(4)
    plane_filter(4)
    mean_field(3)
    mean_field(0)
    from_neighbours(1)
    plane_filter(1)
    parts = parts_of(0, 1)
    mean_t, rim_t = flat_mean(3)
    first_rim, z_t, *planes = own_plane(
        [rim_product(window(4)), mean_t, *parts[:3], parts[3] + rim_t]
    )
    first_rim = pack_rims(first_rim)
    (second_t,) = own_span(3, [z_t], [pack_rims(planes[3])])
    shared = (first_rim, second_t, *own_mean(3))
    component(0, 1, planes, *shared)
    from_neighbours(2)
    plane_filter(2)
    for i in (1, 2):
        mean_field(i)
        component(i, 3, own_plane(parts_of(i, 3)), *shared)

    place = zi * 2 * ROW + xi * 2 + s
    st_in[place] = st[...]
    for device in mates:
        remote(st.at[0:3], st_in.at[place, 0:3], a_s.at[0], a_r.at[0], device).start()
    both_edges.wait_send()
    own = x.at[:, 1, pl.ds(mine, 8)]
    remote(own, own, z_s.at[0], z_r.at[0], {"stream": o}).wait_send()
    for side in range(2):

        @pl.when(wl < nw - 1 if side == 0 else wl > 0)
        def _(side=side):
            remote(
                x.at[:, 1], x.at[:, 2 * side], y_s.at[side], y_r.at[0, side], (above, below)[side]
            ).wait_send()

    several = st_in.at[0 : len(mates), 0:3]
    all_sums = remote(several, several, a_s.at[0], a_r.at[0], mates[0])
    all_sums.wait_recv()
    total = st_in[0, 0:3]
    for k in range(1, len(mates) + 1):
        total = total + st_in[k, 0:3]
    sums_out[0:3, :] = total
    sums_out[3:8, :] = jnp.zeros((5, 128), F32)

    all_sums.wait_send()


def finish(
    cells, clark, similar, sums, clark_out, similar_out, cc_out, sc_out,
    c_buf, s_buf, cc_buf, sc_buf, sem,
):
    total = sums[0:3, 0:80] / cells
    power_e, power_c, power_s = total[:, 32:48], total[:, 48:64], total[:, 64:80]
    copies = []

    def send(src, dst):
        copy = pltpu.make_async_copy(src, dst, sem.at[len(copies)])
        copy.start()
        copies.append(copy)

    spot = lax.broadcasted_iota(jnp.int32, (16, 16), 0) == lax.broadcasted_iota(
        jnp.int32, (16, 16), 1
    )
    for power, values, buf, out in (
        (power_c, clark, c_buf, clark_out), (power_s, similar, s_buf, similar_out)
    ):
        scale = 1.0 / jnp.sqrt(power + small_eps)
        for i in range(3):
            rows = jnp.where(spot, jnp.broadcast_to(scale[i : i + 1], (16, 16)), 0.0)
            rows = jnp.broadcast_to(jnp.sum(rows, axis=1, keepdims=True), (16, 128))
            buf[i] = values[i] * rows[None]
        send(buf, out)
    cc_buf[...] = total[:, 0:16] / jnp.sqrt((power_e + small_eps) * (power_c + small_eps))
    send(cc_buf, cc_out)
    sc_buf[...] = total[:, 16:32] / jnp.sqrt((power_e + small_eps) * (power_s + small_eps))
    send(sc_buf, sc_out)
    for copy in copies:
        copy.wait()


def shards(fields):
    nz = lax.axis_size("span") // ROW
    cells = float(
        fields.shape[1] * fields.shape[3] * lax.axis_size("stream") * lax.axis_size("span")
    )
    km, ko = plane_matrices()
    wm = span_matrices()
    vmem = pl.BlockSpec(memory_space=pltpu.VMEM)
    hbm = pl.BlockSpec(memory_space=pltpu.HBM)
    dma = pltpu.SemaphoreType.DMA

    flux = jax.ShapeDtypeStruct((3, 8, 16, 128), F32)
    corr = jax.ShapeDtypeStruct((3, 16), F32)
    clark, similar, sums = pl.pallas_call(
        kernel,
        out_shape=(flux, flux, jax.ShapeDtypeStruct((8, 128), F32)),
        in_specs=[hbm] * 4,
        out_specs=(vmem, vmem, vmem),
        scratch_shapes=[
            pltpu.VMEM((NQ, 3, 16, 16, 128), F32),
            pltpu.VMEM((2, 8, 8, 128), F32),
            pltpu.VMEM((2, 8, 8, 128), F32),
            pltpu.VMEM((2, 128, 768), BF),
            pltpu.VMEM((128, 1536), BF),
            pltpu.VMEM((4, 512, 256), BF),
            pltpu.VMEM((4, 512, 128), BF),
            pltpu.VMEM((4, 512, 128), BF),
            pltpu.VMEM((4, 512, 128), BF),
            pltpu.VMEM((4, 18, 32, 128), F32),
            pltpu.VMEM((4, 16, 32, 128), F32),
            pltpu.VMEM((8, 128), F32),
            pltpu.VMEM((2 * ROW * nz, 8, 128), F32),
            dma((4,)),
            dma((1,)), dma((NQ,)),
            dma((2,)), dma((NQ, 2)),
            dma((1,)), dma((1,)),
            dma((1,)), dma((1,)),
        ],
        compiler_params=pltpu.CompilerParams(
            collective_id=0, has_side_effects=True, vmem_limit_bytes=54680 * 2**10
        ),
        cost_estimate=pl.CostEstimate(
            flops=8_000_000_000, bytes_accessed=4_000_000, transcendentals=0
        ),
    )(fields, jnp.asarray(km), jnp.asarray(ko), jnp.asarray(wm))

    def last(*refs):
        finish(cells, *refs)

    return pl.pallas_call(
        last,
        out_shape=(flux, flux, corr, corr),
        in_specs=[vmem] * 3,
        out_specs=(hbm, hbm, hbm, hbm),
        scratch_shapes=[
            pltpu.VMEM((3, 8, 16, 128), F32),
            pltpu.VMEM((3, 8, 16, 128), F32),
            pltpu.VMEM((3, 16), F32),
            pltpu.VMEM((3, 16), F32),
            dma((4,)),
        ],
        compiler_params=pltpu.CompilerParams(vmem_limit_bytes=8 * 2**20),
    )(clark, similar, sums)


def solution(mesh):
    return jax.shard_map(
        shards,
        mesh=mesh,
        in_specs=(P(None, "stream", "wall", "span"),),
        out_specs=(
            P(None, "stream", "wall", "span"),
            P(None, "stream", "wall", "span"),
            P(None, "wall"),
            P(None, "wall"),
        ),
        check_vma=False,
    )
```

```python
import math

import jax
import jax.numpy as jnp
import ml_dtypes
import numpy as np
from jax import lax
from jax.experimental import pallas as pl
from jax.experimental.pallas import tpu as pltpu
from jax.sharding import PartitionSpec as P

raw_taps = [math.exp(-((k - 8) ** 2) / 18.0) for k in range(17)]
filter_taps = [value / sum(raw_taps) for value in raw_taps]
clark_coef = 9.0
small_eps = 1e-06

MESH = pl.DeviceIdType.MESH
BF = jnp.bfloat16
F32 = jnp.float32
ROW = 4
NQ = 5


def tap(out_at, in_at):
    offset = in_at - out_at + 8
    inside = (offset >= 0) & (offset <= 16)
    return np.where(inside, np.array(filter_taps)[np.clip(offset, 0, 16)], 0.0)


def split(matrix):
    full = matrix.astype(np.float32)
    hi = full.astype(ml_dtypes.bfloat16)
    lo = (full - hi.astype(np.float32)).astype(ml_dtypes.bfloat16)
    return hi, lo


def left_stack(matrix):
    hi, lo = split(matrix)
    return np.concatenate([hi, hi, lo], axis=1)


def plane_matrices():
    near, w_out = np.meshgrid(np.arange(8), np.arange(16), indexing="ij")
    near, w_out = near.reshape(-1, 1), w_out.reshape(-1, 1)
    b, s, w = np.meshgrid(np.arange(2), np.arange(8), np.arange(16), indexing="ij")
    wall = tap(w_out + 8, (b * 16 + w).reshape(1, -1)) * 0.5
    direct, mirror = tap(near, s.reshape(1, -1)), tap(near, 15 - s.reshape(1, -1))
    folded = np.stack([left_stack((direct + mirror) * wall), left_stack((direct - mirror) * wall)])
    s_out, w_out = np.meshgrid(np.arange(16), np.arange(16), indexing="ij")
    s_out, w_out = s_out.reshape(-1, 1), w_out.reshape(-1, 1)
    s, w = np.meshgrid(np.arange(16), np.arange(32), indexing="ij")
    rows = tap(s_out, s.reshape(1, -1)) * tap(w_out + 8, w.reshape(1, -1))
    own = np.stack([left_stack(rows[:128]), left_stack(rows[128:])])
    return folded, own


def span_matrices():
    lane = np.arange(128)
    group, inner = lane // 32, lane % 32
    place = np.where(inner < 16, inner - 16, inner + 112)
    kept = (inner >= 8) & (inner < 24)
    result = []
    for f in range(4):
        columns = np.concatenate([lane, place])
        used = np.concatenate([lane >= 0, (group == f) & kept])
        cells = tap(columns[None, :], lane[:, None]) * used[None, :]
        rims = tap(columns[None, :], place[:32, None]) * used[None, :]
        (cell_hi, cell_lo), (rim_hi, rim_lo) = split(cells), split(rims)
        packed = np.zeros((128, 256), ml_dtypes.bfloat16)
        for k, part in enumerate((rim_hi, rim_hi, rim_lo)):
            at = 32 * ((f + k) % 4)
            packed[at : at + 32] = part
        result.append(np.concatenate([cell_hi, cell_hi, cell_lo, packed]))
    return np.stack(result)


def hi_lo(values):
    hi = values.astype(BF)
    return hi, (values - hi.astype(F32)).astype(BF)


def pack_rims(rims):
    hi = rims.astype(BF).astype(F32)
    group = lax.broadcasted_iota(jnp.int32, rims.shape, 1) // 32
    low, again = pltpu.roll(rims - hi, 32, 1), pltpu.roll(hi, 64, 1)

    def of_field(f):
        packed = jnp.where(group == f, hi, jnp.where(group == (f + 1) % 4, low, again))
        return packed.astype(BF)

    return of_field


def rim_product(rims):
    lane = lax.broadcasted_iota(jnp.int32, rims.shape, 1)
    last = jnp.where(lane >= 96, rims, 0.0)
    last = last + pltpu.roll(last, 32, 1)
    last = last + pltpu.roll(last, 64, 1)
    return rims * last


def kernel(
    fields, km_in, ko_in, w_in,
    clark_out, similar_out, sums_out,
    x, edge, edge_in, km, ko, wm, yh, yl, ys, m, mh, st, st_in,
    loc, z_s, z_r, y_s, y_r, e_s, e_r, a_s, a_r,
):
    p, wl, s = lax.axis_index("span"), lax.axis_index("wall"), lax.axis_index("stream")
    np_, nw = lax.axis_size("span"), lax.axis_size("wall")
    nz = np_ // ROW
    xi, zi = p % ROW, p // ROW
    o = 1 - s
    mine = pl.multiple_of(s * 8, 8)
    theirs = pl.multiple_of(o * 8, 8)

    mates = [
        {"span": ((zi + k // 8) % nz) * ROW + (xi + k % 8 // 2) % ROW, "stream": (s + k % 2) % 2}
        for k in sorted(range(1, 8 * nz), key=lambda k: -min(k // 8, nz - k // 8))
    ]
    ahead, behind = {"span": (p + 1) % np_}, {"span": (p + np_ - 1) % np_}
    above, below = {"wall": (wl + 1) % nw}, {"wall": (wl + nw - 1) % nw}
    greet = mates + [above, below]

    barrier = pltpu.get_barrier_semaphore()
    for device in greet:
        pl.semaphore_signal(barrier, inc=1, device_id=device, device_id_type=MESH)

    local = [
        pltpu.make_async_copy(fields, x.at[0:4, 1, pl.ds(mine, 8)], loc.at[0]),
        pltpu.make_async_copy(km_in, km, loc.at[1]),
        pltpu.make_async_copy(ko_in.at[s], ko, loc.at[2]),
        pltpu.make_async_copy(w_in, wm, loc.at[3]),
    ]
    for copy in local:
        copy.start()

    @pl.when(wl == 0)
    def _():
        x[:, 0] = jnp.zeros((NQ, 16, 16, 128), F32)

    @pl.when(wl == nw - 1)
    def _():
        x[:, 2] = jnp.zeros((NQ, 16, 16, 128), F32)

    local[0].wait()

    lane = lax.broadcasted_iota(jnp.int32, (64, 128), 1)
    to_next = jnp.zeros((64, 128), F32)
    to_prev = jnp.zeros((64, 128), F32)
    for f in range(4):
        for half in range(2):
            part = x[f, 1, pl.ds(mine, 8), 8 * half : 8 * half + 8, :].reshape(64, 128)
            at = f * 32 + 16 * half
            here = (lane >= at) & (lane < at + 16)
            to_next = jnp.where(here, pltpu.roll(part, (at - 112) % 128, 1), to_next)
            at = f * 32 + 16 * (1 - half)
            here = (lane >= at) & (lane < at + 16)
            to_prev = jnp.where(here, pltpu.roll(part, at % 128, 1) if at else part, to_prev)
    edge[0] = to_next.reshape(8, 8, 128)
    edge[1] = to_prev.reshape(8, 8, 128)

    pl.semaphore_wait(barrier, len(greet))

    def remote(src, dst, send, recv, device):
        return pltpu.make_async_remote_copy(
            src, dst, send, recv, device_id=device, device_id_type=MESH
        )

    def across(q):
        own = x.at[q, 1, pl.ds(mine, 8)]
        return remote(own, own, z_s.at[0], z_r.at[q], {"stream": o})

    def along(q, side, layers):
        return remote(
            x.at[q, 1, layers], x.at[q, 2 * side, layers],
            y_s.at[side], y_r.at[q, side], (above, below)[side],
        )

    def to_neighbours(q, layers):
        for side in (1, 0):

            @pl.when(wl < nw - 1 if side == 0 else wl > 0)
            def _(side=side):
                along(q, side, pl.ds(layers, 8)).start()

    def from_neighbours(q):
        for side in range(2):

            @pl.when(wl > 0 if side == 0 else wl < nw - 1)
            def _(side=side):
                along(q, side, pl.ds(0, 16)).wait_recv()

    def send_own(q):
        across(q).start()
        to_neighbours(q, mine)

    def forward(q):
        across(q).wait_recv()
        to_neighbours(q, theirs)

    def plane_filter(q):
        folds = ([], [])
        for b in range(3):
            near = x[q, b, 0:8]
            far = jnp.concatenate([x[q, b, 15 - k : 16 - k] for k in range(8)], axis=0)
            folds[0].append(hi_lo((near + far).reshape(128, 128)))
            folds[1].append(hi_lo((near - far).reshape(128, 128)))

        def pair(blocks, k):
            return jnp.concatenate(
                [
                    jnp.concatenate([blocks[0][k], blocks[1][k]], axis=0),
                    jnp.concatenate([blocks[1][k], blocks[2][k]], axis=0),
                ],
                axis=1,
            )

        even, odd = [
            jnp.dot(
                km[k],
                jnp.concatenate([pair(fold, 0), pair(fold, 1), pair(fold, 0)], axis=0),
                preferred_element_type=F32,
            )
            for k, fold in enumerate(folds)
        ]
        near, far = even + odd, even - odd
        for half in range(2):
            lanes = slice(128 * half, 128 * half + 128)
            y = jnp.concatenate(
                [near[:, lanes]] + [far[112 - 16 * k : 128 - 16 * k, lanes] for k in range(8)],
                axis=0,
            )
            rows = slice(256 * half, 256 * half + 256)
            if q == 4:
                of_field = pack_rims(y)
                for f in range(4):
                    ys[f, rows, :] = of_field(f)
            else:
                yh[q, rows, :], yl[q, rows, :] = hi_lo(y)

    low = jnp.where(wl > 0, 1.0, 0.0)
    high = jnp.where(wl < nw - 1, 1.0, 0.0)

    def mean_field(f):
        out = jnp.dot(
            jnp.concatenate([yh[f], yl[f], yh[f], ys[f]], axis=1),
            wm[f],
            preferred_element_type=F32,
        ).reshape(2, 16, 16, 256)
        parts = (out[0, :, 0:8] * low, out[0, :, 8:16], out[1, :, 0:8], out[1, :, 8:16] * high)
        for k in range(4):
            m[f, 1:17, 8 * k : 8 * k + 8, :] = parts[k][:, :, :128]
            mh[f, :, 8 * k : 8 * k + 8, :] = parts[k][:, :, 128:]

    def window(q):
        return jnp.concatenate(
            [x[q, 0, :, 8:16, :], x[q, 1], x[q, 2, :, 0:8, :]], axis=1
        ).reshape(512, 128)

    def own_plane(values):
        hi, lo = hi_lo(jnp.concatenate(values, axis=1))
        out = jnp.dot(
            ko[...], jnp.concatenate([hi, lo, hi], axis=0), preferred_element_type=F32
        )
        return [out[:, 128 * k : 128 * k + 128] for k in range(len(values))]

    def own_span(f, bodies, rims):
        hi, lo = hi_lo(jnp.concatenate(bodies, axis=0))
        rim = jnp.concatenate([of_field(f) for of_field in rims], axis=0)
        out = jnp.dot(
            jnp.concatenate([hi, lo, hi, rim], axis=1),
            wm[f, :, 0:128],
            preferred_element_type=F32,
        )
        return [out[128 * k : 128 * k + 128] for k in range(len(bodies))]

    inner = pl.ds(1 + s * 8, 8)
    wide = lax.broadcasted_iota(jnp.int32, (128, 128), 1)

    def own_mean(f):
        c = m[f, inner, 8:24, :].reshape(128, 128)
        rim = mh[f, pl.ds(mine, 8), 8:24, :].reshape(128, 128)
        up = pltpu.roll(c, 127, 1)
        up = jnp.where(wide == 127, pltpu.roll(rim, (127 - (f * 32 + 16)) % 128, 1), up)
        down = pltpu.roll(c, 1, 1)
        down = jnp.where(wide == 0, pltpu.roll(rim, (128 - (f * 32 + 15)) % 128, 1), down)
        along_wall = m[f, inner, 9:25, :] - m[f, inner, 7:23, :]
        along_stream = m[f, pl.ds(2 + s * 8, 8), 8:24, :] - m[f, pl.ds(s * 8, 8), 8:24, :]
        return c, (
            (up - down) * 0.5,
            along_wall.reshape(128, 128) * 0.5,
            along_stream.reshape(128, 128) * 0.5,
        )

    def flat_mean(f):
        return m[f, 1:17].reshape(512, 128), mh[f].reshape(512, 128)

    ones = jnp.ones((8, 384), BF)

    def parts_of(i, place):
        mean, rim = flat_mean(i)
        mean_t, rim_t = flat_mean(3)
        product_rim = rim * pltpu.roll(rim_t, (32 * i - 96) % 128, 1)
        both = rim + pltpu.roll(product_rim, 32 * (place - i) % 128, 1)
        return [window(i) * window(3), mean, mean * mean_t, both]

    def component(i, place, planes, first_rim, second_t, own_t, slopes_t):
        z_x, z_m, z_p, z_r = planes
        z_r = pack_rims(z_r)
        first, second = own_span(i, [z_x, z_m], [first_rim, z_r])
        (flux,) = own_span(place, [z_p], [z_r])
        own, slopes = own_mean(i)
        exact = first - own * own_t
        similar = flux - second * second_t
        total = slopes[0] * slopes_t[0] + slopes[1] * slopes_t[1]
        clark = clark_coef * (total + slopes[2] * slopes_t[2])
        clark_out[i] = clark.reshape(8, 16, 128)
        similar_out[i] = similar.reshape(8, 16, 128)
        pairs = (
            (exact, clark), (exact, similar), (exact, exact), (clark, clark), (similar, similar)
        )
        rows = [jnp.sum((a * b).reshape(8, 16, 128), axis=0) for a, b in pairs]
        rows = jnp.concatenate(rows, axis=0)
        high = rows.astype(BF)
        middle, low = hi_lo(rows - high.astype(F32))
        got = lax.dot_general(
            ones, jnp.concatenate([high, middle, low], axis=1), (((1,), (1,)), ((), ())),
            preferred_element_type=F32,
        )
        st[i : i + 1, 0:80] = got[0:1, :]

    for k, device in enumerate((ahead, behind)):
        remote(edge.at[k], edge_in.at[k], e_s.at[0], e_r.at[0], device).start()
    across(3).start()
    across(0).start()
    for q in (3, 0):
        to_neighbours(q, mine)

    both_edges = remote(edge, edge_in, e_s.at[0], e_r.at[0], ahead)
    both_edges.wait_recv()
    before = edge_in[0].reshape(64, 128)
    after = edge_in[1].reshape(64, 128)
    left = lane % 32 < 16
    x[4, 1, pl.ds(mine, 8), 0:8, :] = jnp.where(left, before, after).reshape(8, 8, 128)
    x[4, 1, pl.ds(mine, 8), 8:16, :] = jnp.where(
        left, pltpu.roll(before, 112, 1), pltpu.roll(after, 16, 1)
    ).reshape(8, 8, 128)
    for q in (4, 1, 2):
        send_own(q)

    st[...] = jnp.zeros((8, 128), F32)
    m[:, 0] = jnp.zeros((4, 32, 128), F32)
    m[:, 17] = jnp.zeros((4, 32, 128), F32)
    forward(3)
    forward(0)
    for copy in local[1:]:
        copy.wait()
    forward(4)
    from_neighbours(3)
    plane_filter(3)
    forward(1)
    from_neighbours(0)
    plane_filter(0)
    forward(2)
    from_neighbours(4)
    plane_filter(4)
    mean_field(3)
    mean_field(0)
    from_neighbours(1)
    plane_filter(1)
    parts = parts_of(0, 1)
    mean_t, rim_t = flat_mean(3)
    first_rim, z_t, *planes = own_plane(
        [rim_product(window(4)), mean_t, *parts[:3], parts[3] + rim_t]
    )
    first_rim = pack_rims(first_rim)
    (second_t,) = own_span(3, [z_t], [pack_rims(planes[3])])
    shared = (first_rim, second_t, *own_mean(3))
    component(0, 1, planes, *shared)
    from_neighbours(2)
    plane_filter(2)
    for i in (1, 2):
        mean_field(i)
        component(i, 3, own_plane(parts_of(i, 3)), *shared)

    place = zi * 2 * ROW + xi * 2 + s
    st_in[place] = st[...]
    for device in mates:
        remote(st.at[0:3], st_in.at[place, 0:3], a_s.at[0], a_r.at[0], device).start()
    both_edges.wait_send()
    own = x.at[:, 1, pl.ds(mine, 8)]
    remote(own, own, z_s.at[0], z_r.at[0], {"stream": o}).wait_send()
    for side in range(2):

        @pl.when(wl < nw - 1 if side == 0 else wl > 0)
        def _(side=side):
            remote(
                x.at[:, 1], x.at[:, 2 * side], y_s.at[side], y_r.at[0, side], (above, below)[side]
            ).wait_send()

    several = st_in.at[0 : len(mates), 0:3]
    all_sums = remote(several, several, a_s.at[0], a_r.at[0], mates[0])
    all_sums.wait_recv()
    total = st_in[0, 0:3]
    for k in range(1, len(mates) + 1):
        total = total + st_in[k, 0:3]
    sums_out[0:3, :] = total
    sums_out[3:8, :] = jnp.zeros((5, 128), F32)

    all_sums.wait_send()


def finish(
    cells, clark, similar, sums, clark_out, similar_out, cc_out, sc_out,
    c_buf, s_buf, cc_buf, sc_buf, sem,
):
    total = sums[0:3, 0:80] / cells
    power_e, power_c, power_s = total[:, 32:48], total[:, 48:64], total[:, 64:80]
    copies = []

    def send(src, dst):
        copy = pltpu.make_async_copy(src, dst, sem.at[len(copies)])
        copy.start()
        copies.append(copy)

    spot = lax.broadcasted_iota(jnp.int32, (16, 16), 0) == lax.broadcasted_iota(
        jnp.int32, (16, 16), 1
    )
    for power, values, buf, out in (
        (power_c, clark, c_buf, clark_out), (power_s, similar, s_buf, similar_out)
    ):
        scale = 1.0 / jnp.sqrt(power + small_eps)
        for i in range(3):
            rows = jnp.where(spot, jnp.broadcast_to(scale[i : i + 1], (16, 16)), 0.0)
            rows = jnp.broadcast_to(jnp.sum(rows, axis=1, keepdims=True), (16, 128))
            buf[i] = values[i] * rows[None]
        send(buf, out)
    cc_buf[...] = total[:, 0:16] / jnp.sqrt((power_e + small_eps) * (power_c + small_eps))
    send(cc_buf, cc_out)
    sc_buf[...] = total[:, 16:32] / jnp.sqrt((power_e + small_eps) * (power_s + small_eps))
    send(sc_buf, sc_out)
    for copy in copies:
        copy.wait()


def shards(fields):
    nz = lax.axis_size("span") // ROW
    cells = float(
        fields.shape[1] * fields.shape[3] * lax.axis_size("stream") * lax.axis_size("span")
    )
    km, ko = plane_matrices()
    wm = span_matrices()
    vmem = pl.BlockSpec(memory_space=pltpu.VMEM)
    hbm = pl.BlockSpec(memory_space=pltpu.HBM)
    dma = pltpu.SemaphoreType.DMA

    flux = jax.ShapeDtypeStruct((3, 8, 16, 128), F32)
    corr = jax.ShapeDtypeStruct((3, 16), F32)
    clark, similar, sums = pl.pallas_call(
        kernel,
        out_shape=(flux, flux, jax.ShapeDtypeStruct((8, 128), F32)),
        in_specs=[hbm] * 4,
        out_specs=(vmem, vmem, vmem),
        scratch_shapes=[
            pltpu.VMEM((NQ, 3, 16, 16, 128), F32),
            pltpu.VMEM((2, 8, 8, 128), F32),
            pltpu.VMEM((2, 8, 8, 128), F32),
            pltpu.VMEM((2, 128, 768), BF),
            pltpu.VMEM((128, 1536), BF),
            pltpu.VMEM((4, 512, 256), BF),
            pltpu.VMEM((4, 512, 128), BF),
            pltpu.VMEM((4, 512, 128), BF),
            pltpu.VMEM((4, 512, 128), BF),
            pltpu.VMEM((4, 18, 32, 128), F32),
            pltpu.VMEM((4, 16, 32, 128), F32),
            pltpu.VMEM((8, 128), F32),
            pltpu.VMEM((2 * ROW * nz, 8, 128), F32),
            dma((4,)),
            dma((1,)), dma((NQ,)),
            dma((2,)), dma((NQ, 2)),
            dma((1,)), dma((1,)),
            dma((1,)), dma((1,)),
        ],
        compiler_params=pltpu.CompilerParams(
            collective_id=0, has_side_effects=True, vmem_limit_bytes=54680 * 2**10
        ),
        cost_estimate=pl.CostEstimate(
            flops=8_000_000_000, bytes_accessed=4_000_000, transcendentals=0
        ),
    )(fields, jnp.asarray(km), jnp.asarray(ko), jnp.asarray(wm))

    def last(*refs):
        finish(cells, *refs)

    return pl.pallas_call(
        last,
        out_shape=(flux, flux, corr, corr),
        in_specs=[vmem] * 3,
        out_specs=(hbm, hbm, hbm, hbm),
        scratch_shapes=[
            pltpu.VMEM((3, 8, 16, 128), F32),
            pltpu.VMEM((3, 8, 16, 128), F32),
            pltpu.VMEM((3, 16), F32),
            pltpu.VMEM((3, 16), F32),
            dma((4,)),
        ],
        compiler_params=pltpu.CompilerParams(vmem_limit_bytes=8 * 2**20),
    )(clark, similar, sums)


def solution(mesh):
    return jax.shard_map(
        shards,
        mesh=mesh,
        in_specs=(P(None, "stream", "wall", "span"),),
        out_specs=(
            P(None, "stream", "wall", "span"),
            P(None, "stream", "wall", "span"),
            P(None, "wall"),
            P(None, "wall"),
        ),
        check_vma=False,
    )
```

```python
import math

import jax
import jax.numpy as jnp
import ml_dtypes
import numpy as np
from jax import lax
from jax.experimental import pallas as pl
from jax.experimental.pallas import tpu as pltpu
from jax.sharding import PartitionSpec as P

raw_taps = [math.exp(-((k - 8) ** 2) / 18.0) for k in range(17)]
filter_taps = [value / sum(raw_taps) for value in raw_taps]
clark_coef = 9.0
small_eps = 1e-06

MESH = pl.DeviceIdType.MESH
BF = jnp.bfloat16
F32 = jnp.float32
ROW = 4
NQ = 5


def tap(out_at, in_at):
    offset = in_at - out_at + 8
    inside = (offset >= 0) & (offset <= 16)
    return np.where(inside, np.array(filter_taps)[np.clip(offset, 0, 16)], 0.0)


def split(matrix):
    full = matrix.astype(np.float32)
    hi = full.astype(ml_dtypes.bfloat16)
    lo = (full - hi.astype(np.float32)).astype(ml_dtypes.bfloat16)
    return hi, lo


def left_stack(matrix):
    hi, lo = split(matrix)
    return np.concatenate([hi, hi, lo], axis=1)


def plane_matrices():
    near, w_out = np.meshgrid(np.arange(8), np.arange(16), indexing="ij")
    near, w_out = near.reshape(-1, 1), w_out.reshape(-1, 1)
    b, s, w = np.meshgrid(np.arange(2), np.arange(8), np.arange(16), indexing="ij")
    wall = tap(w_out + 8, (b * 16 + w).reshape(1, -1)) * 0.5
    direct, mirror = tap(near, s.reshape(1, -1)), tap(near, 15 - s.reshape(1, -1))
    folded = np.stack([left_stack((direct + mirror) * wall), left_stack((direct - mirror) * wall)])
    s_out, w_out = np.meshgrid(np.arange(16), np.arange(16), indexing="ij")
    s_out, w_out = s_out.reshape(-1, 1), w_out.reshape(-1, 1)
    s, w = np.meshgrid(np.arange(16), np.arange(32), indexing="ij")
    rows = tap(s_out, s.reshape(1, -1)) * tap(w_out + 8, w.reshape(1, -1))
    own = np.stack([left_stack(rows[:128]), left_stack(rows[128:])])
    return folded, own


def span_matrices():
    lane = np.arange(128)
    group, inner = lane // 32, lane % 32
    place = np.where(inner < 16, inner - 16, inner + 112)
    kept = (inner >= 8) & (inner < 24)
    result = []
    for f in range(4):
        columns = np.concatenate([lane, place])
        used = np.concatenate([lane >= 0, (group == f) & kept])
        cells = tap(columns[None, :], lane[:, None]) * used[None, :]
        rims = tap(columns[None, :], place[:32, None]) * used[None, :]
        (cell_hi, cell_lo), (rim_hi, rim_lo) = split(cells), split(rims)
        packed = np.zeros((128, 256), ml_dtypes.bfloat16)
        for k, part in enumerate((rim_hi, rim_hi, rim_lo)):
            at = 32 * ((f + k) % 4)
            packed[at : at + 32] = part
        result.append(np.concatenate([cell_hi, cell_hi, cell_lo, packed]))
    return np.stack(result)


def hi_lo(values):
    hi = values.astype(BF)
    return hi, (values - hi.astype(F32)).astype(BF)


def pack_rims(rims):
    hi = rims.astype(BF).astype(F32)
    group = lax.broadcasted_iota(jnp.int32, rims.shape, 1) // 32
    low, again = pltpu.roll(rims - hi, 32, 1), pltpu.roll(hi, 64, 1)

    def of_field(f):
        packed = jnp.where(group == f, hi, jnp.where(group == (f + 1) % 4, low, again))
        return packed.astype(BF)

    return of_field


def rim_product(rims):
    lane = lax.broadcasted_iota(jnp.int32, rims.shape, 1)
    last = jnp.where(lane >= 96, rims, 0.0)
    last = last + pltpu.roll(last, 32, 1)
    last = last + pltpu.roll(last, 64, 1)
    return rims * last


def kernel(
    fields, km_in, ko_in, w_in,
    clark_out, similar_out, sums_out,
    x, edge, edge_in, km, ko, wm, yh, yl, ys, m, mh, st, st_in,
    loc, z_s, z_r, y_s, y_r, e_s, e_r, a_s, a_r,
):
    p, wl, s = lax.axis_index("span"), lax.axis_index("wall"), lax.axis_index("stream")
    np_, nw = lax.axis_size("span"), lax.axis_size("wall")
    nz = np_ // ROW
    xi, zi = p % ROW, p // ROW
    o = 1 - s
    mine = pl.multiple_of(s * 8, 8)
    theirs = pl.multiple_of(o * 8, 8)

    mates = [
        {"span": ((zi + k // 8) % nz) * ROW + (xi + k % 8 // 2) % ROW, "stream": (s + k % 2) % 2}
        for k in sorted(range(1, 8 * nz), key=lambda k: -min(k // 8, nz - k // 8))
    ]
    ahead, behind = {"span": (p + 1) % np_}, {"span": (p + np_ - 1) % np_}
    above, below = {"wall": (wl + 1) % nw}, {"wall": (wl + nw - 1) % nw}
    greet = mates + [above, below]

    barrier = pltpu.get_barrier_semaphore()
    for device in greet:
        pl.semaphore_signal(barrier, inc=1, device_id=device, device_id_type=MESH)

    local = [
        pltpu.make_async_copy(fields, x.at[0:4, 1, pl.ds(mine, 8)], loc.at[0]),
        pltpu.make_async_copy(km_in, km, loc.at[1]),
        pltpu.make_async_copy(ko_in.at[s], ko, loc.at[2]),
        pltpu.make_async_copy(w_in, wm, loc.at[3]),
    ]
    for copy in local:
        copy.start()

    @pl.when(wl == 0)
    def _():
        x[:, 0] = jnp.zeros((NQ, 16, 16, 128), F32)

    @pl.when(wl == nw - 1)
    def _():
        x[:, 2] = jnp.zeros((NQ, 16, 16, 128), F32)

    local[0].wait()

    lane = lax.broadcasted_iota(jnp.int32, (64, 128), 1)
    to_next = jnp.zeros((64, 128), F32)
    to_prev = jnp.zeros((64, 128), F32)
    for f in range(4):
        for half in range(2):
            part = x[f, 1, pl.ds(mine, 8), 8 * half : 8 * half + 8, :].reshape(64, 128)
            at = f * 32 + 16 * half
            here = (lane >= at) & (lane < at + 16)
            to_next = jnp.where(here, pltpu.roll(part, (at - 112) % 128, 1), to_next)
            at = f * 32 + 16 * (1 - half)
            here = (lane >= at) & (lane < at + 16)
            to_prev = jnp.where(here, pltpu.roll(part, at % 128, 1) if at else part, to_prev)
    edge[0] = to_next.reshape(8, 8, 128)
    edge[1] = to_prev.reshape(8, 8, 128)

    pl.semaphore_wait(barrier, len(greet))

    def remote(src, dst, send, recv, device):
        return pltpu.make_async_remote_copy(
            src, dst, send, recv, device_id=device, device_id_type=MESH
        )

    def across(q, half):
        own = x.at[q, 1, pl.ds(mine + 4 * half, 4)]
        return remote(own, own, z_s.at[0], z_r.at[q, half], {"stream": o})

    def along(q, side, layers):
        return remote(
            x.at[q, 1, layers], x.at[q, 2 * side, layers],
            y_s.at[side], y_r.at[q, side], (above, below)[side],
        )

    def to_neighbours(q, start, count):
        for side in (1, 0):

            @pl.when(wl < nw - 1 if side == 0 else wl > 0)
            def _(side=side):
                along(q, side, pl.ds(start, count)).start()

    def from_neighbours(q):
        for side in range(2):

            @pl.when(wl > 0 if side == 0 else wl < nw - 1)
            def _(side=side):
                along(q, side, pl.ds(0, 16)).wait_recv()

    def send_own(q):
        for half in range(2):
            across(q, half).start()
        to_neighbours(q, mine, 8)

    def forward(q):
        for half in range(2):
            across(q, half).wait_recv()
            to_neighbours(q, theirs + 4 * half, 4)

    def plane_filter(q):
        folds = ([], [])
        for b in range(3):
            near = x[q, b, 0:8]
            far = jnp.concatenate([x[q, b, 15 - k : 16 - k] for k in range(8)], axis=0)
            folds[0].append(hi_lo((near + far).reshape(128, 128)))
            folds[1].append(hi_lo((near - far).reshape(128, 128)))

        def pair(blocks, k):
            return jnp.concatenate(
                [
                    jnp.concatenate([blocks[0][k], blocks[1][k]], axis=0),
                    jnp.concatenate([blocks[1][k], blocks[2][k]], axis=0),
                ],
                axis=1,
            )

        even, odd = [
            jnp.dot(
                km[k],
                jnp.concatenate([pair(fold, 0), pair(fold, 1), pair(fold, 0)], axis=0),
                preferred_element_type=F32,
            )
            for k, fold in enumerate(folds)
        ]
        near, far = even + odd, even - odd
        for half in range(2):
            lanes = slice(128 * half, 128 * half + 128)
            y = jnp.concatenate(
                [near[:, lanes]] + [far[112 - 16 * k : 128 - 16 * k, lanes] for k in range(8)],
                axis=0,
            )
            rows = slice(256 * half, 256 * half + 256)
            if q == 4:
                of_field = pack_rims(y)
                for f in range(4):
                    ys[f, rows, :] = of_field(f)
            else:
                yh[q, rows, :], yl[q, rows, :] = hi_lo(y)

    low = jnp.where(wl > 0, 1.0, 0.0)
    high = jnp.where(wl < nw - 1, 1.0, 0.0)

    def mean_field(f):
        out = jnp.dot(
            jnp.concatenate([yh[f], yl[f], yh[f], ys[f]], axis=1),
            wm[f],
            preferred_element_type=F32,
        ).reshape(2, 16, 16, 256)
        parts = (out[0, :, 0:8] * low, out[0, :, 8:16], out[1, :, 0:8], out[1, :, 8:16] * high)
        for k in range(4):
            m[f, 1:17, 8 * k : 8 * k + 8, :] = parts[k][:, :, :128]
            mh[f, :, 8 * k : 8 * k + 8, :] = parts[k][:, :, 128:]

    def window(q):
        return jnp.concatenate(
            [x[q, 0, :, 8:16, :], x[q, 1], x[q, 2, :, 0:8, :]], axis=1
        ).reshape(512, 128)

    def own_plane(values):
        hi, lo = hi_lo(jnp.concatenate(values, axis=1))
        out = jnp.dot(
            ko[...], jnp.concatenate([hi, lo, hi], axis=0), preferred_element_type=F32
        )
        return [out[:, 128 * k : 128 * k + 128] for k in range(len(values))]

    def own_span(f, bodies, rims):
        hi, lo = hi_lo(jnp.concatenate(bodies, axis=0))
        rim = jnp.concatenate([of_field(f) for of_field in rims], axis=0)
        out = jnp.dot(
            jnp.concatenate([hi, lo, hi, rim], axis=1),
            wm[f, :, 0:128],
            preferred_element_type=F32,
        )
        return [out[128 * k : 128 * k + 128] for k in range(len(bodies))]

    inner = pl.ds(1 + s * 8, 8)
    wide = lax.broadcasted_iota(jnp.int32, (128, 128), 1)

    def own_mean(f):
        c = m[f, inner, 8:24, :].reshape(128, 128)
        rim = mh[f, pl.ds(mine, 8), 8:24, :].reshape(128, 128)
        up = pltpu.roll(c, 127, 1)
        up = jnp.where(wide == 127, pltpu.roll(rim, (127 - (f * 32 + 16)) % 128, 1), up)
        down = pltpu.roll(c, 1, 1)
        down = jnp.where(wide == 0, pltpu.roll(rim, (128 - (f * 32 + 15)) % 128, 1), down)
        along_wall = m[f, inner, 9:25, :] - m[f, inner, 7:23, :]
        along_stream = m[f, pl.ds(2 + s * 8, 8), 8:24, :] - m[f, pl.ds(s * 8, 8), 8:24, :]
        return c, (
            (up - down) * 0.5,
            along_wall.reshape(128, 128) * 0.5,
            along_stream.reshape(128, 128) * 0.5,
        )

    def flat_mean(f):
        return m[f, 1:17].reshape(512, 128), mh[f].reshape(512, 128)

    ones = jnp.ones((8, 128), F32)

    def parts_of(i, place):
        mean, rim = flat_mean(i)
        mean_t, rim_t = flat_mean(3)
        product_rim = rim * pltpu.roll(rim_t, (32 * i - 96) % 128, 1)
        both = rim + pltpu.roll(product_rim, 32 * (place - i) % 128, 1)
        return [window(i) * window(3), mean, mean * mean_t, both]

    def component(i, place, planes, first_rim, second_t, own_t, slopes_t):
        z_x, z_m, z_p, z_r = planes
        z_r = pack_rims(z_r)
        first, second = own_span(i, [z_x, z_m], [first_rim, z_r])
        (flux,) = own_span(place, [z_p], [z_r])
        own, slopes = own_mean(i)
        exact = first - own * own_t
        similar = flux - second * second_t
        total = slopes[0] * slopes_t[0] + slopes[1] * slopes_t[1]
        clark = clark_coef * (total + slopes[2] * slopes_t[2])
        clark_out[i] = clark.reshape(8, 16, 128)
        similar_out[i] = similar.reshape(8, 16, 128)
        pairs = (
            (exact, clark), (exact, similar), (exact, exact), (clark, clark), (similar, similar)
        )
        rows = [jnp.sum((a * b).reshape(8, 16, 128), axis=0) for a, b in pairs]
        got = lax.dot_general(
            ones, jnp.concatenate(rows, axis=0), (((1,), (1,)), ((), ())),
            precision=lax.Precision.HIGHEST, preferred_element_type=F32,
        )
        st[i : i + 1, 0:80] = got[0:1, :]

    for k, device in enumerate((ahead, behind)):
        remote(edge.at[k], edge_in.at[k], e_s.at[0], e_r.at[0], device).start()
    for q in (3, 0):
        for half in range(2):
            across(q, half).start()
    for q in (3, 0):
        to_neighbours(q, mine, 8)

    both_edges = remote(edge, edge_in, e_s.at[0], e_r.at[0], ahead)
    both_edges.wait_recv()
    before = edge_in[0].reshape(64, 128)
    after = edge_in[1].reshape(64, 128)
    left = lane % 32 < 16
    x[4, 1, pl.ds(mine, 8), 0:8, :] = jnp.where(left, before, after).reshape(8, 8, 128)
    x[4, 1, pl.ds(mine, 8), 8:16, :] = jnp.where(
        left, pltpu.roll(before, 112, 1), pltpu.roll(after, 16, 1)
    ).reshape(8, 8, 128)
    for q in (4, 1, 2):
        send_own(q)

    st[...] = jnp.zeros((8, 128), F32)
    m[:, 0] = jnp.zeros((4, 32, 128), F32)
    m[:, 17] = jnp.zeros((4, 32, 128), F32)
    forward(3)
    forward(0)
    for copy in local[1:]:
        copy.wait()
    forward(4)
    from_neighbours(3)
    plane_filter(3)
    forward(1)
    from_neighbours(0)
    plane_filter(0)
    forward(2)
    from_neighbours(4)
    plane_filter(4)
    mean_field(3)
    mean_field(0)
    from_neighbours(1)
    plane_filter(1)
    parts = parts_of(0, 1)
    mean_t, rim_t = flat_mean(3)
    first_rim, z_t, *planes = own_plane(
        [rim_product(window(4)), mean_t, *parts[:3], parts[3] + rim_t]
    )
    first_rim = pack_rims(first_rim)
    (second_t,) = own_span(3, [z_t], [pack_rims(planes[3])])
    shared = (first_rim, second_t, *own_mean(3))
    component(0, 1, planes, *shared)
    from_neighbours(2)
    plane_filter(2)
    for i in (1, 2):
        mean_field(i)
        component(i, 3, own_plane(parts_of(i, 3)), *shared)

    place = zi * 2 * ROW + xi * 2 + s
    st_in[place] = st[...]
    for device in mates:
        remote(st.at[0:3], st_in.at[place, 0:3], a_s.at[0], a_r.at[0], device).start()
    both_edges.wait_send()
    own = x.at[:, 1, pl.ds(mine, 8)]
    remote(own, own, z_s.at[0], z_r.at[0, 0], {"stream": o}).wait_send()
    for side in range(2):

        @pl.when(wl < nw - 1 if side == 0 else wl > 0)
        def _(side=side):
            remote(
                x.at[:, 1], x.at[:, 2 * side], y_s.at[side], y_r.at[0, side], (above, below)[side]
            ).wait_send()

    several = st_in.at[0 : len(mates), 0:3]
    all_sums = remote(several, several, a_s.at[0], a_r.at[0], mates[0])
    all_sums.wait_recv()
    total = st_in[0, 0:3]
    for k in range(1, len(mates) + 1):
        total = total + st_in[k, 0:3]
    sums_out[0:3, :] = total
    sums_out[3:8, :] = jnp.zeros((5, 128), F32)

    all_sums.wait_send()


def finish(
    cells, clark, similar, sums, clark_out, similar_out, cc_out, sc_out,
    c_buf, s_buf, cc_buf, sc_buf, sem,
):
    total = sums[0:3, 0:80] / cells
    power_e, power_c, power_s = total[:, 32:48], total[:, 48:64], total[:, 64:80]
    copies = []

    def send(src, dst):
        copy = pltpu.make_async_copy(src, dst, sem.at[len(copies)])
        copy.start()
        copies.append(copy)

    spot = lax.broadcasted_iota(jnp.int32, (16, 16), 0) == lax.broadcasted_iota(
        jnp.int32, (16, 16), 1
    )
    for power, values, buf, out in (
        (power_c, clark, c_buf, clark_out), (power_s, similar, s_buf, similar_out)
    ):
        scale = 1.0 / jnp.sqrt(power + small_eps)
        for i in range(3):
            rows = jnp.where(spot, jnp.broadcast_to(scale[i : i + 1], (16, 16)), 0.0)
            rows = jnp.broadcast_to(jnp.sum(rows, axis=1, keepdims=True), (16, 128))
            buf[i] = values[i] * rows[None]
        send(buf, out)
    cc_buf[...] = total[:, 0:16] / jnp.sqrt((power_e + small_eps) * (power_c + small_eps))
    send(cc_buf, cc_out)
    sc_buf[...] = total[:, 16:32] / jnp.sqrt((power_e + small_eps) * (power_s + small_eps))
    send(sc_buf, sc_out)
    for copy in copies:
        copy.wait()


def shards(fields):
    nz = lax.axis_size("span") // ROW
    cells = float(
        fields.shape[1] * fields.shape[3] * lax.axis_size("stream") * lax.axis_size("span")
    )
    km, ko = plane_matrices()
    wm = span_matrices()
    vmem = pl.BlockSpec(memory_space=pltpu.VMEM)
    hbm = pl.BlockSpec(memory_space=pltpu.HBM)
    dma = pltpu.SemaphoreType.DMA

    flux = jax.ShapeDtypeStruct((3, 8, 16, 128), F32)
    corr = jax.ShapeDtypeStruct((3, 16), F32)
    clark, similar, sums = pl.pallas_call(
        kernel,
        out_shape=(flux, flux, jax.ShapeDtypeStruct((8, 128), F32)),
        in_specs=[hbm] * 4,
        out_specs=(vmem, vmem, vmem),
        scratch_shapes=[
            pltpu.VMEM((NQ, 3, 16, 16, 128), F32),
            pltpu.VMEM((2, 8, 8, 128), F32),
            pltpu.VMEM((2, 8, 8, 128), F32),
            pltpu.VMEM((2, 128, 768), BF),
            pltpu.VMEM((128, 1536), BF),
            pltpu.VMEM((4, 512, 256), BF),
            pltpu.VMEM((4, 512, 128), BF),
            pltpu.VMEM((4, 512, 128), BF),
            pltpu.VMEM((4, 512, 128), BF),
            pltpu.VMEM((4, 18, 32, 128), F32),
            pltpu.VMEM((4, 16, 32, 128), F32),
            pltpu.VMEM((8, 128), F32),
            pltpu.VMEM((2 * ROW * nz, 8, 128), F32),
            dma((4,)),
            dma((1,)), dma((NQ, 2)),
            dma((2,)), dma((NQ, 2)),
            dma((1,)), dma((1,)),
            dma((1,)), dma((1,)),
        ],
        compiler_params=pltpu.CompilerParams(
            collective_id=0, has_side_effects=True, vmem_limit_bytes=54680 * 2**10
        ),
        cost_estimate=pl.CostEstimate(
            flops=8_000_000_000, bytes_accessed=4_000_000, transcendentals=0
        ),
    )(fields, jnp.asarray(km), jnp.asarray(ko), jnp.asarray(wm))

    def last(*refs):
        finish(cells, *refs)

    return pl.pallas_call(
        last,
        out_shape=(flux, flux, corr, corr),
        in_specs=[vmem] * 3,
        out_specs=(hbm, hbm, hbm, hbm),
        scratch_shapes=[
            pltpu.VMEM((3, 8, 16, 128), F32),
            pltpu.VMEM((3, 8, 16, 128), F32),
            pltpu.VMEM((3, 16), F32),
            pltpu.VMEM((3, 16), F32),
            dma((4,)),
        ],
        compiler_params=pltpu.CompilerParams(vmem_limit_bytes=8 * 2**20),
    )(clark, similar, sums)


def solution(mesh):
    return jax.shard_map(
        shards,
        mesh=mesh,
        in_specs=(P(None, "stream", "wall", "span"),),
        out_specs=(
            P(None, "stream", "wall", "span"),
            P(None, "stream", "wall", "span"),
            P(None, "wall"),
            P(None, "wall"),
        ),
        check_vma=False,
    )
```
